32 devices in a mesh: groups: 2 (over y), ctx: 16 (over z, x, core).
Axes of the slice: x: 2, y: 2, z: 4, core: 2. Of those that a mesh axis runs over, the one named last changes fastest.
Arguments:
- outer_gate: bfloat16 [32768, 256], P(('groups', 'ctx')), parts along dimension 0, may hold values from -6 to 6
- inner_gate: bfloat16 [32768, 256], P(('groups', 'ctx')), parts along dimension 0, may hold values from -6 to 6
- values: bfloat16 [32768, 256], P(('groups', 'ctx')), parts along dimension 0, may hold values from -6 to 6
- cotangent: bfloat16 [32768, 256], P(('groups', 'ctx')), parts along dimension 0, may hold values from -6 to 6
- residue: float32 [256, 16], replicated, may hold values from -0.5 to 0.5
- decay_rate: float32 [256, 16], replicated, may hold values from 1.8310547e-05 to 0.1
- skip_gain: float32 [256], replicated, may hold values from -4 to 4
Outputs:
- layer_out: bfloat16 [32768, 256], P(('groups', 'ctx')), parts along dimension 0
- grad_outer: bfloat16 [32768, 256], P(('groups', 'ctx')), parts along dimension 0
- grad_inner: bfloat16 [32768, 256], P(('groups', 'ctx')), parts along dimension 0
- grad_values: bfloat16 [32768, 256], P(('groups', 'ctx')), parts along dimension 0
The draws below stay inside these ranges and needn't reach their ends.
There are 2 independent parts, one for each index of `groups`. The reference program is written for one: setup_inputs(seed, part) draws one part's arguments, and reference() takes and returns one part's arrays. A program takes and returns all parts, laid end to end along the dimension named above; an argument that names none is the same for every part. Nothing has to cross between parts.
All inputs are finite; a program needn't handle non-finite values.
Results may differ from the reference program's by a relative error of at most 0.005.
Values sent between devices are 32-bit elements; how exact they have to be, the bound alone decides.
No kernel may reach another device: no remote copies, remote signals or barrier semaphores. Data moves between devices by JAX's collectives and lax.ppermute only.
A program may use at most 128 MiB of HBM per device.

```python
import math
import jax
import jax.numpy as jnp
from jax import lax

TOK_DEV = 1024
CHANNELS = 256
POLE_COUNT = 16
TOKENS = 16384


def pole_draws(key):
    base_key = jax.random.fold_in(key, 7)
    pick_key, slow_key, middle_key, fast_key, sign_key = jax.random.split(base_key, 5)
    slow_share = 0.5
    middle_share = 0.3
    grid_shape = (CHANNELS, POLE_COUNT)
    slow_rates = jnp.exp(jax.random.uniform(slow_key, grid_shape, jnp.float32, math.log(0.3 / TOKENS), math.log(2.0 / TOKENS)))
    middle_low = min(0.5 / TOK_DEV, 0.05)
    middle_high = min(4.0 / TOK_DEV, 0.1)
    middle_rates = jnp.exp(jax.random.uniform(middle_key, grid_shape, jnp.float32, math.log(middle_low), math.log(middle_high)))
    fast_rates = jnp.exp(jax.random.uniform(fast_key, grid_shape, jnp.float32, math.log(0.02), math.log(0.1)))
    ticket = jax.random.uniform(pick_key, grid_shape, jnp.float32)
    rates = jnp.where(ticket < slow_share, slow_rates, jnp.where(ticket < slow_share + middle_share, middle_rates, fast_rates))
    amplitude = jnp.clip(jax.random.normal(sign_key, grid_shape, jnp.float32), -4.0, 4.0)
    energy = -jnp.expm1(-2.0 * rates * TOKENS) / (2.0 * rates)
    residues = amplitude / jnp.sqrt(POLE_COUNT * energy)
    return (rates.astype(jnp.float32), residues.astype(jnp.float32))


def draw_decay_rate(key, part):
    rates, residues = pole_draws(key)
    return rates


def draw_residue(key, part):
    rates, residues = pole_draws(key)
    return residues


def block_scale(rng, dims, pieces, smallest, top_value):
    gain, own = 1.0, jax.random.fold_in(rng, 6)
    for position, parts in pieces:
        steps = jnp.exp(jax.random.uniform(jax.random.fold_in(own, position), (parts,), jnp.float32, smallest / len(pieces), top_value / len(pieces)))
        gain = gain * jnp.repeat(steps, dims[position] // parts).reshape([-1 if axis == position else 1 for axis in range(len(dims))])
    return gain


def gaussian(key, shape, spread, reach, cuts=(), kind=jnp.bfloat16):
    loudness = block_scale(key, shape, cuts, -0.22, 0.18) if cuts else 1.0
    entries = jax.random.normal(key, shape, jnp.float32) * spread * loudness
    return jnp.minimum(jnp.maximum(entries, -reach), reach).astype(kind)


def setup_inputs(seed: int = 0, part: int = 0) -> dict:
    key_list = jax.random.split(jax.random.key(seed), 8)
    part_splits = jax.random.split(jax.random.fold_in(key_list[7], part), 8)
    return {
        "outer_gate": gaussian(part_splits[0], (TOKENS, CHANNELS), 1.0, 6.0, ((0, 16),)),
        "inner_gate": gaussian(part_splits[1], (TOKENS, CHANNELS), 1.0, 6.0, ((0, 16),)),
        "values": gaussian(part_splits[2], (TOKENS, CHANNELS), 1.0, 6.0, ((0, 16),)),
        "cotangent": gaussian(part_splits[3], (TOKENS, CHANNELS), 1.0, 6.0, ((0, 16),)),
        "residue": draw_residue(jax.random.fold_in(key_list[7], 71), part),
        "decay_rate": draw_decay_rate(jax.random.fold_in(key_list[7], 71), part),
        "skip_gain": gaussian(key_list[6], (CHANNELS,), 1.0, 4.0, (), jnp.float32),
    }


def filters(residue, decay_rate, length):
    lag_steps = jnp.arange(length, dtype=jnp.float32)
    taps_all = jnp.zeros((length, residue.shape[0]), jnp.float32)
    for pole_index in range(POLE_COUNT):
        taps_all = taps_all + residue[:, pole_index][None, :] * jnp.exp(-decay_rate[:, pole_index][None, :] * lag_steps[:, None])
    return taps_all


def causal_conv(signal, taps_all):
    length = signal.shape[0]
    spectrum = jnp.fft.rfft(signal, n=2 * length, axis=0) * jnp.fft.rfft(taps_all, n=2 * length, axis=0)
    return jnp.fft.irfft(spectrum, n=2 * length, axis=0)[:length]


def reference(outer_gate, inner_gate, values, cotangent, residue, decay_rate, skip_gain):
    length = TOKENS
    mixed_input = (inner_gate.astype(jnp.float32) * values.astype(jnp.float32)).astype(jnp.bfloat16)
    mixed_float = lax.optimization_barrier(mixed_input).astype(jnp.float32)
    taps_all = filters(residue, decay_rate, length)
    response = skip_gain[None, :] * mixed_float + causal_conv(mixed_float, taps_all)
    layer_out = (outer_gate.astype(jnp.float32) * response).astype(jnp.bfloat16)
    grad_outer = (cotangent.astype(jnp.float32) * response).astype(jnp.bfloat16)
    grad_response = outer_gate.astype(jnp.float32) * cotangent.astype(jnp.float32)
    adjoint = causal_conv(grad_response[::-1], taps_all)[::-1]
    grad_mixed = skip_gain[None, :] * grad_response + adjoint
    grad_inner = (grad_mixed * values.astype(jnp.float32)).astype(jnp.bfloat16)
    grad_values = (grad_mixed * inner_gate.astype(jnp.float32)).astype(jnp.bfloat16)
    return (layer_out, grad_outer, grad_inner, grad_values)
```

```python
import functools
import jax
import jax.numpy as jnp
from jax import lax
from jax.experimental import pallas as pl
from jax.experimental.pallas import tpu as pltpu
from jax.sharding import PartitionSpec as P

SEGS = 8
LANES = 128
PAD = 8
F32 = jnp.float32
BF16 = jnp.bfloat16
VMEM = pl.BlockSpec(memory_space=pltpu.VMEM)
HBM = pl.BlockSpec(memory_space=pltpu.HBM)


def half_slices(channels):
    return [slice(h, h + LANES) for h in range(0, channels, LANES)]


def rows_at(index, pitch):
    return pl.ds(index, SEGS, stride=pitch)


def state_kernel(
    seg_len,
    outer_hbm,
    inner_hbm,
    values_hbm,
    cotangent_hbm,
    rate_ref,
    residue_ref,
    mixed_ref,
    grad_ref,
    ends_ref,
    starts_ref,
    own_ref,
    table_ref,
    outer_ref,
    inner_ref,
    values_ref,
    cotangent_ref,
    copy_sems,
):
    rows, channels = inner_ref.shape
    poles = rate_ref.shape[0]
    pitch = seg_len + PAD
    halves = half_slices(channels)
    pairs = (
        (inner_hbm, inner_ref),
        (values_hbm, values_ref),
        (outer_hbm, outer_ref),
        (cotangent_hbm, cotangent_ref),
    )
    copies = []
    for h, lanes in enumerate(halves):
        line = []
        for j, (source, target) in enumerate(pairs):
            copy = pltpu.make_async_copy(
                source.at[:, lanes], target.at[:, lanes], copy_sems.at[h, j]
            )
            copy.start()
            line.append(copy)
        copies.append(line)
    rate_table = rate_ref[...]
    table_ref[0:poles, :] = rate_table
    table_ref[poles : 2 * poles, :] = residue_ref[...]
    decay = jnp.exp(-rate_table)
    seg_index = lax.broadcasted_iota(jnp.int32, (SEGS, LANES), 0).astype(F32)
    for h, lanes in enumerate(halves):
        for copy in copies[h]:
            copy.wait()
        for q in range(SEGS):
            source = slice(q * seg_len, (q + 1) * seg_len)
            target = slice(q * pitch, q * pitch + seg_len)
            mixed = inner_ref[source, lanes].astype(F32) * values_ref[source, lanes].astype(F32)
            mixed_ref[h, target, :] = mixed.astype(BF16).astype(F32)
            grad_ref[h, target, :] = outer_ref[source, lanes].astype(F32) * cotangent_ref[
                source, lanes
            ].astype(F32)
        steps = [jnp.broadcast_to(decay[k : k + 1, lanes], (SEGS, LANES)) for k in range(poles)]

        def body(i, carry):
            ahead, back = carry
            x = mixed_ref[h, rows_at(i, pitch), :]
            g = grad_ref[h, rows_at(seg_len - 1 - i, pitch), :]
            ahead = tuple(steps[k] * ahead[k] + x for k in range(poles))
            back = tuple(steps[k] * back[k] + g for k in range(poles))
            return ahead, back

        zero = jnp.zeros((SEGS, LANES), F32)
        start = (tuple(zero for _ in range(poles)),) * 2
        ahead, back = lax.fori_loop(0, seg_len, body, start, unroll=8)
        for k in range(poles):
            ends_ref[k, :, lanes] = ahead[k]
            starts_ref[k, :, lanes] = back[k]
            rate = jnp.broadcast_to(rate_table[k : k + 1, lanes], (SEGS, LANES))
            to_end = jnp.exp(-rate * (seg_len * (SEGS - 1.0 - seg_index)))
            to_start = jnp.exp(-rate * (seg_len * seg_index))
            own_ref[k : k + 1, lanes] = jnp.sum(to_end * ahead[k], axis=0, keepdims=True)
            own_ref[poles + k : poles + k + 1, lanes] = jnp.sum(
                to_start * back[k], axis=0, keepdims=True
            )


def local_kernel(seg_len, backward, half, signal_ref, table_ref, skip_ref, out_ref):
    poles = table_ref.shape[0] // 2
    pitch = seg_len + PAD
    lanes = slice(half * LANES, (half + 1) * LANES)
    decay = jnp.exp(-table_ref[0:poles, lanes])
    steps = [jnp.broadcast_to(decay[k : k + 1], (SEGS, LANES)) for k in range(poles)]
    weights = [
        jnp.broadcast_to(table_ref[poles + k : poles + k + 1, lanes], (SEGS, LANES))
        for k in range(poles)
    ]
    skip = jnp.broadcast_to(skip_ref[0:1, lanes], (SEGS, LANES))

    def body(i, states):
        row = seg_len - 1 - i if backward else i
        x = signal_ref[half, rows_at(row, pitch), :]
        states = tuple(steps[k] * states[k] + x for k in range(poles))
        terms = [weights[k] * states[k] for k in range(poles)] + [skip * x]
        while len(terms) > 1:
            terms = [a + b for a, b in zip(terms[::2], terms[1::2])] + (
                [terms[-1]] if len(terms) % 2 else []
            )
        out_ref[rows_at(row, pitch), :] = terms[0]
        return states

    zero = jnp.zeros((SEGS, LANES), F32)
    lax.fori_loop(0, seg_len, body, tuple(zero for _ in range(poles)), unroll=8)


def final_kernel(
    seg_len,
    outer_hbm,
    inner_hbm,
    values_hbm,
    cotangent_hbm,
    ends_ref,
    starts_ref,
    table_ref,
    entry_ref,
    *rest,
):
    channels = table_ref.shape[1]
    halves = half_slices(channels)
    count = len(halves)
    outer_ref, inner_ref, values_ref, cotangent_ref, in_sems = rest[2 * count + 9 :]
    loads = {}
    for h, lanes in enumerate(halves):
        for backward, pairs in (
            (False, ((outer_hbm, outer_ref), (cotangent_hbm, cotangent_ref))),
            (True, ((values_hbm, values_ref), (inner_hbm, inner_ref))),
        ):
            loads[h, backward] = [
                pltpu.make_async_copy(
                    source.at[:, lanes], target.at[:, lanes], in_sems.at[h, 2 * backward + j]
                )
                for j, (source, target) in enumerate(pairs)
            ]
            for copy in loads[h, backward]:
                copy.start()
    ahead_refs, back_refs = rest[:count], rest[count : 2 * count]
    layer_hbm, outer_grad_hbm, inner_grad_hbm, values_grad_hbm = rest[2 * count : 2 * count + 4]
    layer_ref, outer_grad_ref, inner_grad_ref, values_grad_ref = rest[2 * count + 4 : 2 * count + 8]
    sems = rest[2 * count + 8]
    poles = table_ref.shape[0] // 2
    pitch = seg_len + PAD
    step = 16
    inside = lax.broadcasted_iota(jnp.int32, (8, LANES), 0).astype(F32)
    copies = []
    for h, lanes in enumerate(halves):
        rates = [
            jnp.broadcast_to(table_ref[k : k + 1, lanes], (8, LANES)) for k in range(poles)
        ]
        weights = [
            jnp.broadcast_to(table_ref[poles + k : poles + k + 1, lanes], (8, LANES))
            for k in range(poles)
        ]
        strides = [jnp.exp(-8.0 * rates[k]) for k in range(poles)]
        for backward in (False, True):
            if backward:
                local_ref, edge_ref = back_refs[h], starts_ref
                pair = (values_ref, inner_ref)
                targets = ((inner_grad_ref, inner_grad_hbm), (values_grad_ref, values_grad_hbm))
                enter = [weights[k] * jnp.exp(-rates[k] * (8.0 - inside)) for k in range(poles)]
            else:
                local_ref, edge_ref = ahead_refs[h], ends_ref
                pair = (outer_ref, cotangent_ref)
                targets = ((layer_ref, layer_hbm), (outer_grad_ref, outer_grad_hbm))
                enter = [weights[k] * jnp.exp(-rates[k] * (inside + 1.0)) for k in range(poles)]
            base = poles if backward else 0
            carried = tuple(
                enter[k] * jnp.broadcast_to(entry_ref[base + k : base + k + 1, lanes], (8, LANES))
                for k in range(poles)
            )

            for copy in loads[h, backward]:
                copy.wait()

            def total(terms):
                terms = list(terms)
                while len(terms) > 1:
                    terms = [a + b for a, b in zip(terms[::2], terms[1::2])] + (
                        [terms[-1]] if len(terms) % 2 else []
                    )
                return terms[0]

            for n in range(SEGS):
                q = SEGS - 1 - n if backward else n

                def body(i, carried):
                    block = (seg_len // step - 1 - i) if backward else i
                    found = [None, None]
                    for sub in (1, 0) if backward else (0, 1):
                        row = pl.multiple_of(q * pitch + block * step + 8 * sub, 8)
                        found[sub] = total(carried + (local_ref[pl.ds(row, 8), :],))
                        carried = tuple(strides[k] * carried[k] for k in range(poles))
                    whole = jnp.concatenate(found, axis=0)
                    rows = pl.ds(pl.multiple_of(q * seg_len + block * step, step), step)
                    for gate_ref, (target, _) in zip(pair, targets):
                        target[rows, lanes] = (gate_ref[rows, lanes].astype(F32) * whole).astype(
                            BF16
                        )
                    return carried

                carried = lax.fori_loop(0, seg_len // step, body, carried, unroll=4)
                if n < SEGS - 1:
                    carried = tuple(
                        carried[k]
                        + enter[k]
                        * jnp.broadcast_to(edge_ref[k, q : q + 1, lanes], (8, LANES))
                        for k in range(poles)
                    )
            for j, (target, hbm) in enumerate(targets):
                copy = pltpu.make_async_copy(
                    target.at[:, lanes], hbm.at[:, lanes], sems.at[h, 2 * backward + j]
                )
                copy.start()
                copies.append(copy)
    for copy in copies:
        copy.wait()


def shards(outer_gate, inner_gate, values, cotangent, residue, decay_rate, skip_gain):
    rows, channels = values.shape
    poles = residue.shape[1]
    seg_len = rows // SEGS
    padded = SEGS * (seg_len + PAD)
    count = channels // LANES
    blocks = lax.axis_size("ctx")
    position = lax.axis_index("ctx")
    gate = jax.ShapeDtypeStruct((rows, channels), BF16)
    limit = pltpu.CompilerParams(vmem_limit_bytes=4 << 20)
    work = rows * channels * poles
    outer_gate, inner_gate, values, cotangent = (
        pltpu.with_memory_space_constraint(x, pltpu.HBM)
        for x in (outer_gate, inner_gate, values, cotangent)
    )
    mixed, grad, ends, starts, own, table = (
        pl.pallas_call(
            functools.partial(state_kernel, seg_len),
            out_shape=[jax.ShapeDtypeStruct((count, padded, LANES), F32)] * 2
            + [jax.ShapeDtypeStruct((poles, SEGS, channels), F32)] * 2
            + [jax.ShapeDtypeStruct((2 * poles, channels), F32)] * 2,
            in_specs=[HBM] * 4 + [VMEM] * 2,
            out_specs=[VMEM] * 6,
            scratch_shapes=[pltpu.VMEM((rows, channels), BF16)] * 4
            + [pltpu.SemaphoreType.DMA((count, 4))],
            compiler_params=limit,
            name="states",
        )(outer_gate, inner_gate, values, cotangent, decay_rate.T, residue.T)
    )
    skip = skip_gain[None, :]

    def local(signal, backward, half, held):
        signal, _ = lax.optimization_barrier((signal, held))
        return pl.pallas_call(
            functools.partial(local_kernel, seg_len, backward, half),
            out_shape=jax.ShapeDtypeStruct((padded, LANES), F32),
            in_specs=[VMEM] * 3,
            out_specs=VMEM,
            compiler_params=limit,
            cost_estimate=pl.CostEstimate(
                flops=work * 4 // count, bytes_accessed=padded * LANES * 8, transcendentals=0
            ),
            name="local",
        )(signal, table, skip)

    rates = table[:poles]
    jobs = [(mixed, False, h) for h in range(count)] + [(grad, True, h) for h in range(count)]
    found = []
    entry = jnp.zeros_like(own)
    reach = 1
    while reach < blocks:
        other = lax.ppermute(own, "ctx", [(i, i ^ reach) for i in range(blocks)])
        pieces = []
        if reach > 1 and jobs:
            pieces.append(local(*jobs.pop(0), own))
        later = (position // reach) % 2 == 1
        place = position % reach
        ahead_shift = (rows * place).astype(F32)
        back_shift = (rows * (reach - 1 - place)).astype(F32)
        entry = entry + other * jnp.concatenate(
            [
                jnp.where(later, jnp.exp(-rates * ahead_shift), 0.0),
                jnp.where(later, 0.0, jnp.exp(-rates * back_shift)),
            ]
        )
        span = jnp.exp(-rates * float(rows * reach))
        early = jnp.concatenate([span, jnp.ones_like(span)])
        late = jnp.concatenate([jnp.ones_like(span), span])
        own = jnp.where(later, late, early) * own + jnp.where(later, early, late) * other
        reach *= 2
        if reach < blocks:
            own, pieces = lax.optimization_barrier((own, pieces))
        found += pieces
    for job in jobs:
        found.append(local(*job, table))
    return pl.pallas_call(
        functools.partial(final_kernel, seg_len),
        out_shape=[gate] * 4,
        in_specs=[HBM] * 4 + [VMEM] * (4 + 2 * count),
        out_specs=[HBM] * 4,
        scratch_shapes=[pltpu.VMEM((rows, channels), BF16)] * 4
        + [pltpu.SemaphoreType.DMA((count, 4))]
        + [pltpu.VMEM((rows, channels), BF16)] * 4
        + [pltpu.SemaphoreType.DMA((count, 4))],
        compiler_params=pltpu.CompilerParams(vmem_limit_bytes=8 << 20),
        name="final",
    )(outer_gate, inner_gate, values, cotangent, ends, starts, table, entry, *found)


def solution(mesh):
    spread = P(("groups", "ctx"), None)
    return jax.shard_map(
        shards,
        mesh=mesh,
        in_specs=(spread,) * 4 + (P(),) * 3,
        out_specs=(spread,) * 4,
        check_vma=False,
    )
```

```python
import functools
import jax
import jax.numpy as jnp
from jax import lax
from jax.experimental import pallas as pl
from jax.experimental.pallas import tpu as pltpu
from jax.sharding import PartitionSpec as P

SEGS = 8
LANES = 128
PAD = 8
STEP = 16
F32 = jnp.float32
BF16 = jnp.bfloat16
VMEM = pl.BlockSpec(memory_space=pltpu.VMEM)
HBM = pl.BlockSpec(memory_space=pltpu.HBM)


def lane_slice(half):
    return slice(half * LANES, (half + 1) * LANES)


def add_up(terms):
    while len(terms) > 1:
        odd = [terms[-1]] if len(terms) % 2 else []
        terms = [a + b for a, b in zip(terms[::2], terms[1::2])] + odd
    return terms[0]


def spread_rows(table, lanes, count):
    return [jnp.broadcast_to(table[k : k + 1, lanes], (8, LANES)) for k in range(count)]


def state_kernel(
    seg_len,
    outer_hbm,
    inner_hbm,
    values_hbm,
    cotangent_hbm,
    rate_hbm,
    residue_hbm,
    mixed_ref,
    grad_ref,
    ends_ref,
    starts_ref,
    own_ref,
    table_ref,
    outer_ref,
    inner_ref,
    values_ref,
    cotangent_ref,
    copy_sems,
    table_sems,
):
    poles = rate_hbm.shape[0]
    pitch = seg_len + PAD
    count = mixed_ref.shape[0]
    tables = [
        pltpu.make_async_copy(
            source, table_ref.at[pl.ds(j * poles, poles), :], table_sems.at[j]
        )
        for j, source in enumerate((rate_hbm, residue_hbm))
    ]
    for copy in tables:
        copy.start()
    pairs = (
        (inner_hbm, inner_ref),
        (values_hbm, values_ref),
        (outer_hbm, outer_ref),
        (cotangent_hbm, cotangent_ref),
    )
    copies = []
    for h in range(count):
        line = []
        for j, (source, target) in enumerate(pairs):
            copy = pltpu.make_async_copy(
                source.at[:, lane_slice(h)], target.at[:, lane_slice(h)], copy_sems.at[h, j]
            )
            copy.start()
            line.append(copy)
        copies.append(line)
    for copy in tables:
        copy.wait()
    rate_table = table_ref[0:poles, :]
    decay = jnp.exp(-rate_table)
    seg_decay = jnp.exp(-float(seg_len) * rate_table)
    for h in range(count):
        lanes = lane_slice(h)
        for copy in copies[h]:
            copy.wait()

        def convert(q, _):
            source = pl.ds(pl.multiple_of(q * seg_len, 16), seg_len)
            target = pl.ds(pl.multiple_of(q * pitch, 8), seg_len)
            mixed = inner_ref[source, lanes].astype(F32) * values_ref[source, lanes].astype(F32)
            mixed_ref[h, target, :] = mixed.astype(BF16).astype(F32)
            outer, cotangent = outer_ref[source, lanes], cotangent_ref[source, lanes]
            grad_ref[h, target, :] = outer.astype(F32) * cotangent.astype(F32)
            return _

        lax.fori_loop(0, SEGS, convert, 0)
        steps = spread_rows(decay, lanes, poles)

        def body(i, carry):
            ahead, back = carry
            x = mixed_ref[h, pl.ds(i, SEGS, stride=pitch), :]
            g = grad_ref[h, pl.ds(seg_len - 1 - i, SEGS, stride=pitch), :]
            ahead = tuple(steps[k] * ahead[k] + x for k in range(poles))
            back = tuple(steps[k] * back[k] + g for k in range(poles))
            return ahead, back

        zero = jnp.zeros((SEGS, LANES), F32)
        start = (tuple(zero for _ in range(poles)),) * 2
        ahead, back = lax.fori_loop(0, seg_len, body, start, unroll=8)
        for k in range(poles):
            ends_ref[h, 8 * k : 8 * k + 8, :] = ahead[k]
            starts_ref[h, 8 * k : 8 * k + 8, :] = back[k]
        ahead = jnp.zeros((poles, LANES), F32)
        back = jnp.zeros((poles, LANES), F32)
        for q in range(SEGS):
            ahead = seg_decay[:, lanes] * ahead + ends_ref[h, pl.ds(q, poles, stride=8), :]
            back = seg_decay[:, lanes] * back + starts_ref[
                h, pl.ds(SEGS - 1 - q, poles, stride=8), :
            ]
        own_ref[0:poles, lanes] = ahead
        own_ref[poles : 2 * poles, lanes] = back


def local_kernel(seg_len, backward, half, signal_ref, table_ref, skip_ref, out_ref):
    poles = table_ref.shape[0] // 2
    pitch = seg_len + PAD
    lanes = lane_slice(half)
    steps = spread_rows(jnp.exp(-table_ref[0:poles, :]), lanes, poles)
    weights = spread_rows(table_ref[poles : 2 * poles, :], lanes, poles)
    skip = jnp.broadcast_to(skip_ref[0:1, lanes], (SEGS, LANES))

    def body(i, states):
        row = seg_len - 1 - i if backward else i
        x = signal_ref[half, pl.ds(row, SEGS, stride=pitch), :]
        states = tuple(steps[k] * states[k] + x for k in range(poles))
        terms = [weights[k] * states[k] for k in range(poles)] + [skip * x]
        out_ref[pl.ds(row, SEGS, stride=pitch), :] = add_up(terms)
        return states

    zero = jnp.zeros((SEGS, LANES), F32)
    lax.fori_loop(0, seg_len, body, tuple(zero for _ in range(poles)), unroll=8)


def finish_way(seg_len, backward, gates, locals_, edge_ref, table_ref, entry_ref, targets, sems):
    poles = table_ref.shape[0] // 2
    pitch = seg_len + PAD
    inside = lax.broadcasted_iota(jnp.int32, (8, LANES), 0).astype(F32)
    reach = 8.0 - inside if backward else inside + 1.0
    blocks = seg_len // STEP
    copies = []
    for h, local_ref in enumerate(locals_):
        lanes = lane_slice(h)
        rates = spread_rows(table_ref[0:poles, :], lanes, poles)
        weights = spread_rows(table_ref[poles : 2 * poles, :], lanes, poles)
        strides = [jnp.exp(-8.0 * rates[k]) for k in range(poles)]
        enter = [weights[k] * jnp.exp(-rates[k] * reach) for k in range(poles)]
        entry = spread_rows(entry_ref[...], lanes, poles)

        def segment(n, carried, local_ref=local_ref, lanes=lanes, h=h):
            q = SEGS - 1 - n if backward else n

            for i in range(blocks):
                block = blocks - 1 - i if backward else i
                found = [None, None]
                for sub in (1, 0) if backward else (0, 1):
                    row = pl.multiple_of(q * pitch + block * STEP + 8 * sub, 8)
                    found[sub] = add_up([*carried, local_ref[pl.ds(row, 8), :]])
                    carried = tuple(strides[k] * carried[k] for k in range(poles))
                whole = jnp.concatenate(found, axis=0)
                rows = pl.ds(pl.multiple_of(q * seg_len + block * STEP, STEP), STEP)
                for gate_ref, (target, _) in zip(gates, targets):
                    target[rows, lanes] = (gate_ref[rows, lanes].astype(F32) * whole).astype(BF16)
            return tuple(
                carried[k]
                + enter[k]
                * jnp.broadcast_to(edge_ref[h, pl.ds(8 * k + q, 1), :], (8, LANES))
                for k in range(poles)
            )

        lax.fori_loop(0, SEGS, segment, tuple(enter[k] * entry[k] for k in range(poles)))
        for j, (target, hbm) in enumerate(targets):
            copy = pltpu.make_async_copy(target.at[:, lanes], hbm.at[:, lanes], sems.at[h, j])
            copy.start()
            copies.append(copy)
    for copy in copies:
        copy.wait()


def load(pairs, sems):
    copies = [
        pltpu.make_async_copy(source, target, sems.at[j])
        for j, (source, target) in enumerate(pairs)
    ]
    for copy in copies:
        copy.start()
    return copies


def settled_kernel(
    seg_len,
    count,
    blocks,
    outer_hbm,
    inner_hbm,
    values_hbm,
    cotangent_hbm,
    ends_ref,
    starts_ref,
    table_ref,
    entry_ref,
    *rest,
):
    locals_ahead, locals_back = rest[:count], rest[count : 2 * count]
    layer_hbm, outer_grad_hbm, inner_grad_hbm, values_grad_hbm, next_a, next_b = rest[
        2 * count : 2 * count + 6
    ]
    gate_a, gate_b, out_a, out_b, load_sems, next_sems, out_sems = rest[2 * count + 6 :]
    later = lax.axis_index("ctx") >= blocks // 2

    def run(backward):
        pairs = [
            ((outer_hbm, gate_a), (cotangent_hbm, gate_b)),
            ((values_hbm, gate_a), (inner_hbm, gate_b)),
        ]
        others = [
            ((outer_hbm, next_a), (cotangent_hbm, next_b)),
            ((values_hbm, next_a), (inner_hbm, next_b)),
        ]
        now = load(pairs[backward], load_sems)
        following = load(others[1 - backward], next_sems)
        for copy in now:
            copy.wait()
        targets = (
            ((out_a, inner_grad_hbm), (out_b, values_grad_hbm))
            if backward
            else ((out_a, layer_hbm), (out_b, outer_grad_hbm))
        )
        finish_way(
            seg_len,
            backward,
            (gate_a, gate_b),
            locals_back if backward else locals_ahead,
            starts_ref if backward else ends_ref,
            table_ref,
            entry_ref,
            targets,
            out_sems,
        )
        for copy in following:
            copy.wait()

    pl.when(later)(functools.partial(run, True))
    pl.when(jnp.logical_not(later))(functools.partial(run, False))


def last_kernel(
    seg_len,
    count,
    blocks,
    gate_a,
    gate_b,
    ends_ref,
    starts_ref,
    table_ref,
    entry_ref,
    *rest,
):
    locals_ahead, locals_back = rest[:count], rest[count : 2 * count]
    layer_hbm, outer_grad_hbm, inner_grad_hbm, values_grad_hbm = rest[
        2 * count + 4 : 2 * count + 8
    ]
    out_a, out_b, out_sems = rest[2 * count + 8 :]
    later = lax.axis_index("ctx") >= blocks // 2

    def run(backward):
        targets = (
            ((out_a, inner_grad_hbm), (out_b, values_grad_hbm))
            if backward
            else ((out_a, layer_hbm), (out_b, outer_grad_hbm))
        )
        finish_way(
            seg_len,
            backward,
            (gate_a, gate_b),
            locals_back if backward else locals_ahead,
            starts_ref if backward else ends_ref,
            table_ref,
            entry_ref,
            targets,
            out_sems,
        )

    pl.when(later)(functools.partial(run, False))
    pl.when(jnp.logical_not(later))(functools.partial(run, True))


def shards(outer_gate, inner_gate, values, cotangent, residue, decay_rate, skip_gain):
    rows, channels = values.shape
    poles = residue.shape[1]
    seg_len = rows // SEGS
    padded = SEGS * (seg_len + PAD)
    count = channels // LANES
    blocks = lax.axis_size("ctx")
    position = lax.axis_index("ctx")
    gate = jax.ShapeDtypeStruct((rows, channels), BF16)
    limit = pltpu.CompilerParams(vmem_limit_bytes=4 << 20)
    work = rows * channels * poles
    dma = pltpu.SemaphoreType.DMA

    def in_hbm(x):
        return pltpu.with_memory_space_constraint(x, pltpu.HBM)

    arrays = [in_hbm(x) for x in (outer_gate, inner_gate, values, cotangent)]
    mixed, grad, ends, starts, own, table = pl.pallas_call(
        functools.partial(state_kernel, seg_len),
        out_shape=[jax.ShapeDtypeStruct((count, padded, LANES), F32)] * 2
        + [jax.ShapeDtypeStruct((count, 8 * poles, LANES), F32)] * 2
        + [jax.ShapeDtypeStruct((2 * poles, channels), F32)] * 2,
        in_specs=[HBM] * 6,
        out_specs=[VMEM] * 6,
        scratch_shapes=[pltpu.VMEM((rows, channels), BF16)] * 4 + [dma((count, 4)), dma((2,))],
        compiler_params=limit,
        name="states",
    )(*arrays, in_hbm(decay_rate.T), in_hbm(residue.T))
    skip = skip_gain[None, :]

    def local(signal, backward, half, held):
        signal, _ = lax.optimization_barrier((signal, held))
        return pl.pallas_call(
            functools.partial(local_kernel, seg_len, backward, half),
            out_shape=jax.ShapeDtypeStruct((padded, LANES), F32),
            in_specs=[VMEM] * 3,
            out_specs=VMEM,
            compiler_params=limit,
            cost_estimate=pl.CostEstimate(
                flops=work * 4 // count, bytes_accessed=padded * LANES * 8, transcendentals=0
            ),
            name="local",
        )(signal, table, skip)

    rates = table[:poles]
    jobs = [(mixed, False, h) for h in range(count)] + [(grad, True, h) for h in range(count)]
    middle = max(blocks.bit_length() - 3, 1)
    share = -(-len(jobs) // middle)
    found = []
    ahead_entry = jnp.zeros((poles, channels), F32)
    back_entry = ahead_entry
    reach = 1
    while reach < blocks // 2:
        other = lax.ppermute(own, "ctx", [(i, i ^ reach) for i in range(blocks)])
        pieces = []
        if reach > 1:
            now, jobs = jobs[:share], jobs[share:]
            pieces = [local(*job, own) for job in now]
        later = (position // reach) % 2 == 1
        place = position % reach
        ahead_shift = jnp.exp(-rates * (rows * place).astype(F32))
        back_shift = jnp.exp(-rates * (rows * (reach - 1 - place)).astype(F32))
        ahead_entry = ahead_entry + jnp.where(later, ahead_shift, 0.0) * other[:poles]
        back_entry = back_entry + jnp.where(later, 0.0, back_shift) * other[poles:]
        span = jnp.exp(-rates * float(rows * reach))
        early = jnp.concatenate([span, jnp.ones_like(span)])
        late = jnp.concatenate([jnp.ones_like(span), span])
        own = jnp.where(later, late, early) * own + jnp.where(later, early, late) * other
        reach *= 2
        if pieces:
            own, pieces = lax.optimization_barrier((own, pieces))
        found += pieces
    found += [local(*job, own) for job in jobs]
    later = position >= reach
    place = position % reach
    sent = jnp.where(later, own[poles:], own[:poles])
    other = lax.ppermute(sent, "ctx", [(i, i ^ reach) for i in range(blocks)])
    *outs, gate_a, gate_b = pl.pallas_call(
        functools.partial(settled_kernel, seg_len, count, blocks),
        out_shape=[gate] * 6,
        in_specs=[HBM] * 4 + [VMEM] * (4 + 2 * count),
        out_specs=[HBM] * 4 + [VMEM] * 2,
        scratch_shapes=[pltpu.VMEM((rows, channels), BF16)] * 4
        + [dma((2,)), dma((2,)), dma((count, 2))],
        compiler_params=limit,
        cost_estimate=pl.CostEstimate(
            flops=work * 2, bytes_accessed=rows * channels * 12, transcendentals=0
        ),
        name="settled",
    )(*arrays, ends, starts, table, jnp.where(later, back_entry, ahead_entry), *found)
    shift = jnp.exp(-rates * (rows * jnp.where(later, place, reach - 1 - place)).astype(F32))
    entry = jnp.where(later, ahead_entry, back_entry) + shift * other
    first = 6 + 2 * count
    return pl.pallas_call(
        functools.partial(last_kernel, seg_len, count, blocks),
        out_shape=[gate] * 4,
        in_specs=[VMEM] * first + [HBM] * 4,
        out_specs=[HBM] * 4,
        input_output_aliases={first + j: j for j in range(4)},
        scratch_shapes=[pltpu.VMEM((rows, channels), BF16)] * 2 + [dma((count, 2))],
        compiler_params=limit,
        name="last",
    )(gate_a, gate_b, ends, starts, table, entry, *found, *outs)


def solution(mesh):
    spread = P(("groups", "ctx"), None)
    return jax.shard_map(
        shards,
        mesh=mesh,
        in_specs=(spread,) * 4 + (P(),) * 3,
        out_specs=(spread,) * 4,
        check_vma=False,
    )
```

```python
import functools
import jax
import jax.numpy as jnp
from jax import lax
from jax.experimental import pallas as pl
from jax.experimental.pallas import tpu as pltpu
from jax.sharding import PartitionSpec as P

SEGS = 8
LANES = 128
PAD = 8
STEP = 16
F32 = jnp.float32
BF16 = jnp.bfloat16
VMEM = pl.BlockSpec(memory_space=pltpu.VMEM)
HBM = pl.BlockSpec(memory_space=pltpu.HBM)


def lane_slice(half):
    return slice(half * LANES, (half + 1) * LANES)


def add_up(terms):
    while len(terms) > 1:
        odd = [terms[-1]] if len(terms) % 2 else []
        terms = [a + b for a, b in zip(terms[::2], terms[1::2])] + odd
    return terms[0]


def spread_rows(table, lanes, count):
    return [jnp.broadcast_to(table[k : k + 1, lanes], (8, LANES)) for k in range(count)]


def state_kernel(
    seg_len,
    outer_hbm,
    inner_hbm,
    values_hbm,
    cotangent_hbm,
    rate_hbm,
    residue_hbm,
    mixed_ref,
    grad_ref,
    ends_ref,
    starts_ref,
    own_ref,
    table_ref,
    outer_ref,
    inner_ref,
    values_ref,
    cotangent_ref,
    copy_sems,
    table_sems,
):
    poles = rate_hbm.shape[0]
    pitch = seg_len + PAD
    count = mixed_ref.shape[0]
    tables = [
        pltpu.make_async_copy(
            source, table_ref.at[pl.ds(j * poles, poles), :], table_sems.at[j]
        )
        for j, source in enumerate((rate_hbm, residue_hbm))
    ]
    for copy in tables:
        copy.start()
    pairs = (
        (inner_hbm, inner_ref),
        (values_hbm, values_ref),
        (outer_hbm, outer_ref),
        (cotangent_hbm, cotangent_ref),
    )
    copies = []
    for h in range(count):
        line = []
        for j, (source, target) in enumerate(pairs):
            copy = pltpu.make_async_copy(
                source.at[:, lane_slice(h)], target.at[:, lane_slice(h)], copy_sems.at[h, j]
            )
            copy.start()
            line.append(copy)
        copies.append(line)
    for copy in tables:
        copy.wait()
    rate_table = table_ref[0:poles, :]
    decay = jnp.exp(-rate_table)
    seg_decay = jnp.exp(-float(seg_len) * rate_table)
    for h in range(count):
        lanes = lane_slice(h)
        for copy in copies[h]:
            copy.wait()

        def convert(q, _):
            source = pl.ds(pl.multiple_of(q * seg_len, 16), seg_len)
            target = pl.ds(pl.multiple_of(q * pitch, 8), seg_len)
            mixed = inner_ref[source, lanes].astype(F32) * values_ref[source, lanes].astype(F32)
            mixed_ref[h, target, :] = mixed.astype(BF16).astype(F32)
            outer, cotangent = outer_ref[source, lanes], cotangent_ref[source, lanes]
            grad_ref[h, target, :] = outer.astype(F32) * cotangent.astype(F32)
            return _

        lax.fori_loop(0, SEGS, convert, 0)
        steps = spread_rows(decay, lanes, poles)

        def body(i, carry):
            ahead, back = carry
            x = mixed_ref[h, pl.ds(i, SEGS, stride=pitch), :]
            g = grad_ref[h, pl.ds(seg_len - 1 - i, SEGS, stride=pitch), :]
            ahead = tuple(steps[k] * ahead[k] + x for k in range(poles))
            back = tuple(steps[k] * back[k] + g for k in range(poles))
            return ahead, back

        zero = jnp.zeros((SEGS, LANES), F32)
        start = (tuple(zero for _ in range(poles)),) * 2
        ahead, back = lax.fori_loop(0, seg_len, body, start, unroll=8)
        for k in range(poles):
            ends_ref[h, 8 * k : 8 * k + 8, :] = ahead[k]
            starts_ref[h, 8 * k : 8 * k + 8, :] = back[k]
        ahead = jnp.zeros((poles, LANES), F32)
        back = jnp.zeros((poles, LANES), F32)
        for q in range(SEGS):
            ahead = seg_decay[:, lanes] * ahead + ends_ref[h, pl.ds(q, poles, stride=8), :]
            back = seg_decay[:, lanes] * back + starts_ref[
                h, pl.ds(SEGS - 1 - q, poles, stride=8), :
            ]
        own_ref[0:poles, lanes] = ahead
        own_ref[poles : 2 * poles, lanes] = back


def local_kernel(seg_len, backward, signal_ref, table_ref, skip_ref, out_ref):
    poles = table_ref.shape[0] // 2
    pitch = seg_len + PAD
    for h in range(signal_ref.shape[0]):
        lanes = lane_slice(h)
        steps = spread_rows(jnp.exp(-table_ref[0:poles, :]), lanes, poles)
        weights = spread_rows(table_ref[poles : 2 * poles, :], lanes, poles)
        skip = jnp.broadcast_to(skip_ref[0:1, lanes], (SEGS, LANES))

        def body(i, states):
            row = seg_len - 1 - i if backward else i
            x = signal_ref[h, pl.ds(row, SEGS, stride=pitch), :]
            states = tuple(steps[k] * states[k] + x for k in range(poles))
            terms = [weights[k] * states[k] for k in range(poles)] + [skip * x]
            out_ref[h, pl.ds(row, SEGS, stride=pitch), :] = add_up(terms)
            return states

        zero = jnp.zeros((SEGS, LANES), F32)
        lax.fori_loop(0, seg_len, body, tuple(zero for _ in range(poles)), unroll=8)


def finish_way(seg_len, backward, gates, local_ref, edge_ref, table_ref, entry_ref, targets, sems):
    poles = table_ref.shape[0] // 2
    pitch = seg_len + PAD
    inside = lax.broadcasted_iota(jnp.int32, (8, LANES), 0).astype(F32)
    reach = 8.0 - inside if backward else inside + 1.0
    blocks = seg_len // STEP
    copies = []
    for h in range(local_ref.shape[0]):
        lanes = lane_slice(h)
        rates = spread_rows(table_ref[0:poles, :], lanes, poles)
        weights = spread_rows(table_ref[poles : 2 * poles, :], lanes, poles)
        strides = [jnp.exp(-8.0 * rates[k]) for k in range(poles)]
        enter = [weights[k] * jnp.exp(-rates[k] * reach) for k in range(poles)]
        entry = spread_rows(entry_ref[...], lanes, poles)

        def segment(n, carried):
            q = SEGS - 1 - n if backward else n

            for i in range(blocks):
                block = blocks - 1 - i if backward else i
                found = [None, None]
                for sub in (1, 0) if backward else (0, 1):
                    row = pl.multiple_of(q * pitch + block * STEP + 8 * sub, 8)
                    found[sub] = add_up([*carried, local_ref[h, pl.ds(row, 8), :]])
                    carried = tuple(strides[k] * carried[k] for k in range(poles))
                whole = jnp.concatenate(found, axis=0)
                rows = pl.ds(pl.multiple_of(q * seg_len + block * STEP, STEP), STEP)
                for gate_ref, (target, _) in zip(gates, targets):
                    target[rows, lanes] = (gate_ref[rows, lanes].astype(F32) * whole).astype(BF16)
            return tuple(
                carried[k]
                + enter[k]
                * jnp.broadcast_to(edge_ref[h, pl.ds(8 * k + q, 1), :], (8, LANES))
                for k in range(poles)
            )

        lax.fori_loop(0, SEGS, segment, tuple(enter[k] * entry[k] for k in range(poles)))
        for j, (target, hbm) in enumerate(targets):
            copy = pltpu.make_async_copy(target.at[:, lanes], hbm.at[:, lanes], sems.at[h, j])
            copy.start()
            copies.append(copy)
    for copy in copies:
        copy.wait()


def load(pairs, sems):
    copies = [
        pltpu.make_async_copy(source, target, sems.at[j])
        for j, (source, target) in enumerate(pairs)
    ]
    for copy in copies:
        copy.start()
    return copies


def settled_kernel(
    seg_len,
    blocks,
    outer_hbm,
    inner_hbm,
    values_hbm,
    cotangent_hbm,
    ends_ref,
    starts_ref,
    table_ref,
    entry_ref,
    ahead_ref,
    back_ref,
    layer_hbm,
    outer_grad_hbm,
    inner_grad_hbm,
    values_grad_hbm,
    next_a,
    next_b,
    gate_a,
    gate_b,
    out_a,
    out_b,
    load_sems,
    next_sems,
    out_sems,
):
    later = lax.axis_index("ctx") >= blocks // 2

    def run(backward):
        pairs = [
            ((outer_hbm, gate_a), (cotangent_hbm, gate_b)),
            ((values_hbm, gate_a), (inner_hbm, gate_b)),
        ]
        others = [
            ((outer_hbm, next_a), (cotangent_hbm, next_b)),
            ((values_hbm, next_a), (inner_hbm, next_b)),
        ]
        now = load(pairs[backward], load_sems)
        following = load(others[1 - backward], next_sems)
        for copy in now:
            copy.wait()
        targets = (
            ((out_a, inner_grad_hbm), (out_b, values_grad_hbm))
            if backward
            else ((out_a, layer_hbm), (out_b, outer_grad_hbm))
        )
        finish_way(
            seg_len,
            backward,
            (gate_a, gate_b),
            back_ref if backward else ahead_ref,
            starts_ref if backward else ends_ref,
            table_ref,
            entry_ref,
            targets,
            out_sems,
        )
        for copy in following:
            copy.wait()

    pl.when(later)(functools.partial(run, True))
    pl.when(jnp.logical_not(later))(functools.partial(run, False))


def last_kernel(
    seg_len,
    blocks,
    gate_a,
    gate_b,
    ends_ref,
    starts_ref,
    table_ref,
    entry_ref,
    ahead_ref,
    back_ref,
    layer_in,
    outer_grad_in,
    inner_grad_in,
    values_grad_in,
    layer_hbm,
    outer_grad_hbm,
    inner_grad_hbm,
    values_grad_hbm,
    out_a,
    out_b,
    out_sems,
):
    later = lax.axis_index("ctx") >= blocks // 2

    def run(backward):
        targets = (
            ((out_a, inner_grad_hbm), (out_b, values_grad_hbm))
            if backward
            else ((out_a, layer_hbm), (out_b, outer_grad_hbm))
        )
        finish_way(
            seg_len,
            backward,
            (gate_a, gate_b),
            back_ref if backward else ahead_ref,
            starts_ref if backward else ends_ref,
            table_ref,
            entry_ref,
            targets,
            out_sems,
        )

    pl.when(later)(functools.partial(run, False))
    pl.when(jnp.logical_not(later))(functools.partial(run, True))


def shards(outer_gate, inner_gate, values, cotangent, residue, decay_rate, skip_gain):
    rows, channels = values.shape
    poles = residue.shape[1]
    seg_len = rows // SEGS
    padded = SEGS * (seg_len + PAD)
    count = channels // LANES
    blocks = lax.axis_size("ctx")
    position = lax.axis_index("ctx")
    gate = jax.ShapeDtypeStruct((rows, channels), BF16)
    limit = pltpu.CompilerParams(vmem_limit_bytes=4 << 20)
    work = rows * channels * poles
    dma = pltpu.SemaphoreType.DMA

    def in_hbm(x):
        return pltpu.with_memory_space_constraint(x, pltpu.HBM)

    arrays = [in_hbm(x) for x in (outer_gate, inner_gate, values, cotangent)]
    mixed, grad, ends, starts, own, table = pl.pallas_call(
        functools.partial(state_kernel, seg_len),
        out_shape=[jax.ShapeDtypeStruct((count, padded, LANES), F32)] * 2
        + [jax.ShapeDtypeStruct((count, 8 * poles, LANES), F32)] * 2
        + [jax.ShapeDtypeStruct((2 * poles, channels), F32)] * 2,
        in_specs=[HBM] * 6,
        out_specs=[VMEM] * 6,
        scratch_shapes=[pltpu.VMEM((rows, channels), BF16)] * 4 + [dma((count, 4)), dma((2,))],
        compiler_params=limit,
        name="states",
    )(*arrays, in_hbm(decay_rate.T), in_hbm(residue.T))
    skip = skip_gain[None, :]

    def local(signal, backward, held):
        signal, _ = lax.optimization_barrier((signal, held))
        return pl.pallas_call(
            functools.partial(local_kernel, seg_len, backward),
            out_shape=jax.ShapeDtypeStruct(signal.shape, F32),
            in_specs=[VMEM] * 3,
            out_specs=VMEM,
            input_output_aliases={0: 0},
            compiler_params=limit,
            cost_estimate=pl.CostEstimate(
                flops=work * 4, bytes_accessed=signal.size * 8, transcendentals=0
            ),
            name="local",
        )(signal, table, skip)

    rates = table[:poles]
    jobs = [(mixed, False), (grad, True)]
    found = []
    ahead_entry = jnp.zeros((poles, channels), F32)
    back_entry = ahead_entry
    reach = 1
    while reach < blocks // 2:
        other = lax.ppermute(own, "ctx", [(i, i ^ reach) for i in range(blocks)])
        pieces = [local(*jobs.pop(0), own)] if reach > 1 and jobs else []
        later = (position // reach) % 2 == 1
        place = position % reach
        ahead_shift = jnp.exp(-rates * (rows * place).astype(F32))
        back_shift = jnp.exp(-rates * (rows * (reach - 1 - place)).astype(F32))
        ahead_entry = ahead_entry + jnp.where(later, ahead_shift, 0.0) * other[:poles]
        back_entry = back_entry + jnp.where(later, 0.0, back_shift) * other[poles:]
        span = jnp.exp(-rates * float(rows * reach))
        early = jnp.concatenate([span, jnp.ones_like(span)])
        late = jnp.concatenate([jnp.ones_like(span), span])
        own = jnp.where(later, late, early) * own + jnp.where(later, early, late) * other
        reach *= 2
        own, ahead_entry, back_entry, pieces = lax.optimization_barrier(
            (own, ahead_entry, back_entry, pieces)
        )
        found += pieces
    found += [local(*job, own) for job in jobs]
    later = position >= reach
    place = position % reach
    sent = jnp.where(later, own[poles:], own[:poles])
    other = lax.ppermute(sent, "ctx", [(i, i ^ reach) for i in range(blocks)])
    *outs, gate_a, gate_b = pl.pallas_call(
        functools.partial(settled_kernel, seg_len, blocks),
        out_shape=[gate] * 6,
        in_specs=[HBM] * 4 + [VMEM] * (6),
        out_specs=[HBM] * 4 + [VMEM] * 2,
        scratch_shapes=[pltpu.VMEM((rows, channels), BF16)] * 4
        + [dma((2,)), dma((2,)), dma((count, 2))],
        compiler_params=limit,
        cost_estimate=pl.CostEstimate(
            flops=work * 2, bytes_accessed=rows * channels * 12, transcendentals=0
        ),
        name="settled",
    )(*arrays, ends, starts, table, jnp.where(later, back_entry, ahead_entry), *found)
    shift = jnp.exp(-rates * (rows * jnp.where(later, place, reach - 1 - place)).astype(F32))
    entry = jnp.where(later, ahead_entry, back_entry) + shift * other
    first = 8
    return pl.pallas_call(
        functools.partial(last_kernel, seg_len, blocks),
        out_shape=[gate] * 4,
        in_specs=[VMEM] * first + [HBM] * 4,
        out_specs=[HBM] * 4,
        input_output_aliases={first + j: j for j in range(4)},
        scratch_shapes=[pltpu.VMEM((rows, channels), BF16)] * 2 + [dma((count, 2))],
        compiler_params=limit,
        name="last",
    )(gate_a, gate_b, ends, starts, table, entry, *found, *outs)


def solution(mesh):
    spread = P(("groups", "ctx"), None)
    return jax.shard_map(
        shards,
        mesh=mesh,
        in_specs=(spread,) * 4 + (P(),) * 3,
        out_specs=(spread,) * 4,
        check_vma=False,
    )
```

```python
import functools
import jax
import jax.numpy as jnp
from jax import lax
from jax.experimental import pallas as pl
from jax.experimental.pallas import tpu as pltpu
from jax.sharding import PartitionSpec as P

SEGS = 8
LANES = 128
PAD = 8
STEP = 16
F32 = jnp.float32
BF16 = jnp.bfloat16
VMEM = pl.BlockSpec(memory_space=pltpu.VMEM)
HBM = pl.BlockSpec(memory_space=pltpu.HBM)


def lane_slice(half):
    return slice(half * LANES, (half + 1) * LANES)


def add_up(terms):
    while len(terms) > 1:
        odd = [terms[-1]] if len(terms) % 2 else []
        terms = [a + b for a, b in zip(terms[::2], terms[1::2])] + odd
    return terms[0]


def spread_rows(table, lanes, count):
    return [jnp.broadcast_to(table[k : k + 1, lanes], (8, LANES)) for k in range(count)]


def state_kernel(
    seg_len,
    outer_hbm,
    inner_hbm,
    values_hbm,
    cotangent_hbm,
    rate_hbm,
    residue_hbm,
    mixed_ref,
    grad_ref,
    ends_ref,
    starts_ref,
    own_ref,
    table_ref,
    outer_ref,
    inner_ref,
    values_ref,
    cotangent_ref,
    copy_sems,
    table_sems,
):
    poles = rate_hbm.shape[0]
    pitch = seg_len + PAD
    count = mixed_ref.shape[0]
    tables = [
        pltpu.make_async_copy(
            source, table_ref.at[pl.ds(j * poles, poles), :], table_sems.at[j]
        )
        for j, source in enumerate((rate_hbm, residue_hbm))
    ]
    for copy in tables:
        copy.start()
    pairs = (
        (inner_hbm, inner_ref),
        (values_hbm, values_ref),
        (outer_hbm, outer_ref),
        (cotangent_hbm, cotangent_ref),
    )
    copies = []
    for h in range(count):
        line = []
        for j, (source, target) in enumerate(pairs):
            copy = pltpu.make_async_copy(
                source.at[:, lane_slice(h)], target.at[:, lane_slice(h)], copy_sems.at[h, j]
            )
            copy.start()
            line.append(copy)
        copies.append(line)
    for copy in tables:
        copy.wait()
    rate_table = table_ref[0:poles, :]
    decay = jnp.exp(-rate_table)
    seg_decay = jnp.exp(-float(seg_len) * rate_table)
    for h in range(count):
        lanes = lane_slice(h)
        for copy in copies[h]:
            copy.wait()

        def convert(q, _):
            source = pl.ds(pl.multiple_of(q * seg_len, 16), seg_len)
            target = pl.ds(pl.multiple_of(q * pitch, 8), seg_len)
            mixed = inner_ref[source, lanes].astype(F32) * values_ref[source, lanes].astype(F32)
            mixed_ref[h, target, :] = mixed.astype(BF16).astype(F32)
            outer, cotangent = outer_ref[source, lanes], cotangent_ref[source, lanes]
            grad_ref[h, target, :] = outer.astype(F32) * cotangent.astype(F32)
            return _

        lax.fori_loop(0, SEGS, convert, 0)
        steps = spread_rows(decay, lanes, poles)

        def body(i, carry):
            ahead, back = carry
            x = mixed_ref[h, pl.ds(i, SEGS, stride=pitch), :]
            g = grad_ref[h, pl.ds(seg_len - 1 - i, SEGS, stride=pitch), :]
            ahead = tuple(steps[k] * ahead[k] + x for k in range(poles))
            back = tuple(steps[k] * back[k] + g for k in range(poles))
            return ahead, back

        zero = jnp.zeros((SEGS, LANES), F32)
        start = (tuple(zero for _ in range(poles)),) * 2
        ahead, back = lax.fori_loop(0, seg_len, body, start, unroll=8)
        for k in range(poles):
            ends_ref[h, 8 * k : 8 * k + 8, :] = ahead[k]
            starts_ref[h, 8 * k : 8 * k + 8, :] = back[k]
        ahead = jnp.zeros((poles, LANES), F32)
        back = jnp.zeros((poles, LANES), F32)
        for q in range(SEGS):
            ahead = seg_decay[:, lanes] * ahead + ends_ref[h, pl.ds(q, poles, stride=8), :]
            back = seg_decay[:, lanes] * back + starts_ref[
                h, pl.ds(SEGS - 1 - q, poles, stride=8), :
            ]
        own_ref[0:poles, lanes] = ahead
        own_ref[poles : 2 * poles, lanes] = back


def local_kernel(seg_len, backward, signal_ref, table_ref, skip_ref, out_ref):
    poles = table_ref.shape[0] // 2
    pitch = seg_len + PAD
    for h in range(signal_ref.shape[0]):
        lanes = lane_slice(h)
        steps = spread_rows(jnp.exp(-table_ref[0:poles, :]), lanes, poles)
        weights = spread_rows(table_ref[poles : 2 * poles, :], lanes, poles)
        skip = jnp.broadcast_to(skip_ref[0:1, lanes], (SEGS, LANES))

        def body(i, states):
            row = seg_len - 1 - i if backward else i
            x = signal_ref[h, pl.ds(row, SEGS, stride=pitch), :]
            states = tuple(steps[k] * states[k] + x for k in range(poles))
            terms = [weights[k] * states[k] for k in range(poles)] + [skip * x]
            out_ref[h, pl.ds(row, SEGS, stride=pitch), :] = add_up(terms)
            return states

        zero = jnp.zeros((SEGS, LANES), F32)
        lax.fori_loop(0, seg_len, body, tuple(zero for _ in range(poles)), unroll=8)


def finish_way(seg_len, backward, gates, local_ref, edge_ref, table_ref, entry_ref, targets, sems):
    poles = table_ref.shape[0] // 2
    pitch = seg_len + PAD
    inside = lax.broadcasted_iota(jnp.int32, (8, LANES), 0).astype(F32)
    reach = 8.0 - inside if backward else inside + 1.0
    blocks = seg_len // STEP
    copies = []
    for h in range(local_ref.shape[0]):
        lanes = lane_slice(h)
        rates = spread_rows(table_ref[0:poles, :], lanes, poles)
        weights = spread_rows(table_ref[poles : 2 * poles, :], lanes, poles)
        strides = [jnp.exp(-8.0 * rates[k]) for k in range(poles)]
        enter = [weights[k] * jnp.exp(-rates[k] * reach) for k in range(poles)]
        entry = spread_rows(entry_ref[...], lanes, poles)

        def segment(n, carried):
            q = SEGS - 1 - n if backward else n

            for i in range(blocks):
                block = blocks - 1 - i if backward else i
                found = [None, None]
                for sub in (1, 0) if backward else (0, 1):
                    row = pl.multiple_of(q * pitch + block * STEP + 8 * sub, 8)
                    found[sub] = add_up([*carried, local_ref[h, pl.ds(row, 8), :]])
                    carried = tuple(strides[k] * carried[k] for k in range(poles))
                whole = jnp.concatenate(found, axis=0)
                rows = pl.ds(pl.multiple_of(q * seg_len + block * STEP, STEP), STEP)
                for gate_ref, (target, _) in zip(gates, targets):
                    target[rows, lanes] = (gate_ref[rows, lanes].astype(F32) * whole).astype(BF16)
            return tuple(
                carried[k]
                + enter[k]
                * jnp.broadcast_to(edge_ref[h, pl.ds(8 * k + q, 1), :], (8, LANES))
                for k in range(poles)
            )

        lax.fori_loop(0, SEGS, segment, tuple(enter[k] * entry[k] for k in range(poles)))
        for j, (target, hbm) in enumerate(targets):
            copy = pltpu.make_async_copy(target.at[:, lanes], hbm.at[:, lanes], sems.at[h, j])
            copy.start()
            copies.append(copy)
    for copy in copies:
        copy.wait()


def load(pairs, sems):
    copies = [
        pltpu.make_async_copy(source, target, sems.at[j])
        for j, (source, target) in enumerate(pairs)
    ]
    for copy in copies:
        copy.start()
    return copies


def settled_kernel(
    seg_len,
    blocks,
    outer_hbm,
    inner_hbm,
    values_hbm,
    cotangent_hbm,
    ends_ref,
    starts_ref,
    table_ref,
    entry_ref,
    ahead_ref,
    back_ref,
    layer_hbm,
    outer_grad_hbm,
    inner_grad_hbm,
    values_grad_hbm,
    next_a,
    next_b,
    gate_a,
    gate_b,
    out_a,
    out_b,
    load_sems,
    next_sems,
    out_sems,
):
    later = lax.axis_index("ctx") >= blocks // 2

    def run(backward):
        pairs = [
            ((outer_hbm, gate_a), (cotangent_hbm, gate_b)),
            ((values_hbm, gate_a), (inner_hbm, gate_b)),
        ]
        others = [
            ((outer_hbm, next_a), (cotangent_hbm, next_b)),
            ((values_hbm, next_a), (inner_hbm, next_b)),
        ]
        now = load(pairs[backward], load_sems)
        following = load(others[1 - backward], next_sems)
        for copy in now:
            copy.wait()
        targets = (
            ((out_a, inner_grad_hbm), (out_b, values_grad_hbm))
            if backward
            else ((out_a, layer_hbm), (out_b, outer_grad_hbm))
        )
        finish_way(
            seg_len,
            backward,
            (gate_a, gate_b),
            back_ref if backward else ahead_ref,
            starts_ref if backward else ends_ref,
            table_ref,
            entry_ref,
            targets,
            out_sems,
        )
        for copy in following:
            copy.wait()

    pl.when(later)(functools.partial(run, True))
    pl.when(jnp.logical_not(later))(functools.partial(run, False))


def last_kernel(
    seg_len,
    blocks,
    gate_a,
    gate_b,
    ends_ref,
    starts_ref,
    table_ref,
    entry_ref,
    ahead_ref,
    back_ref,
    layer_in,
    outer_grad_in,
    inner_grad_in,
    values_grad_in,
    layer_hbm,
    outer_grad_hbm,
    inner_grad_hbm,
    values_grad_hbm,
    out_a,
    out_b,
    out_sems,
):
    later = lax.axis_index("ctx") >= blocks // 2

    def run(backward):
        targets = (
            ((out_a, inner_grad_hbm), (out_b, values_grad_hbm))
            if backward
            else ((out_a, layer_hbm), (out_b, outer_grad_hbm))
        )
        finish_way(
            seg_len,
            backward,
            (gate_a, gate_b),
            back_ref if backward else ahead_ref,
            starts_ref if backward else ends_ref,
            table_ref,
            entry_ref,
            targets,
            out_sems,
        )

    pl.when(later)(functools.partial(run, False))
    pl.when(jnp.logical_not(later))(functools.partial(run, True))


def shards(outer_gate, inner_gate, values, cotangent, residue, decay_rate, skip_gain):
    rows, channels = values.shape
    poles = residue.shape[1]
    seg_len = rows // SEGS
    padded = SEGS * (seg_len + PAD)
    count = channels // LANES
    blocks = lax.axis_size("ctx")
    position = lax.axis_index("ctx")
    gate = jax.ShapeDtypeStruct((rows, channels), BF16)
    limit = pltpu.CompilerParams(vmem_limit_bytes=4 << 20)
    work = rows * channels * poles
    dma = pltpu.SemaphoreType.DMA

    def in_hbm(x):
        return pltpu.with_memory_space_constraint(x, pltpu.HBM)

    arrays = [in_hbm(x) for x in (outer_gate, inner_gate, values, cotangent)]
    mixed, grad, ends, starts, own, table = pl.pallas_call(
        functools.partial(state_kernel, seg_len),
        out_shape=[jax.ShapeDtypeStruct((count, padded, LANES), F32)] * 2
        + [jax.ShapeDtypeStruct((count, 8 * poles, LANES), F32)] * 2
        + [jax.ShapeDtypeStruct((2 * poles, channels), F32)] * 2,
        in_specs=[HBM] * 6,
        out_specs=[VMEM] * 6,
        scratch_shapes=[pltpu.VMEM((rows, channels), BF16)] * 4 + [dma((count, 4)), dma((2,))],
        compiler_params=limit,
        name="states",
    )(*arrays, in_hbm(decay_rate.T), in_hbm(residue.T))
    skip = skip_gain[None, :]

    def local(signal, backward, held):
        signal, _ = lax.optimization_barrier((signal, held))
        return pl.pallas_call(
            functools.partial(local_kernel, seg_len, backward),
            out_shape=jax.ShapeDtypeStruct(signal.shape, F32),
            in_specs=[VMEM] * 3,
            out_specs=VMEM,
            input_output_aliases={0: 0},
            compiler_params=limit,
            cost_estimate=pl.CostEstimate(
                flops=work * 4, bytes_accessed=signal.size * 8, transcendentals=0
            ),
            name="local",
        )(signal, table, skip)

    rates = table[:poles]
    jobs = [(mixed, False), (grad, True)]
    found = []
    ahead_entry = jnp.zeros((poles, channels), F32)
    back_entry = ahead_entry
    reach = 1
    while reach < blocks // 2:
        other = lax.ppermute(own, "ctx", [(i, i ^ reach) for i in range(blocks)])
        pieces = [local(*jobs.pop(0), own)] if reach > 1 and jobs else []
        later = (position // reach) % 2 == 1
        place = position % reach
        ahead_shift = jnp.exp(-rates * (rows * place).astype(F32))
        back_shift = jnp.exp(-rates * (rows * (reach - 1 - place)).astype(F32))
        ahead_entry = ahead_entry + jnp.where(later, ahead_shift, 0.0) * other[:poles]
        back_entry = back_entry + jnp.where(later, 0.0, back_shift) * other[poles:]
        span = jnp.exp(-rates * float(rows * reach))
        early = jnp.concatenate([span, jnp.ones_like(span)])
        late = jnp.concatenate([jnp.ones_like(span), span])
        own = jnp.where(later, late, early) * own + jnp.where(later, early, late) * other
        reach *= 2
        own, ahead_entry, back_entry, pieces = lax.optimization_barrier(
            (own, ahead_entry, back_entry, pieces)
        )
        found += pieces
    found += [local(*job, own) for job in jobs]
    later = position >= reach
    place = position % reach
    sent = jnp.where(later, own[poles:], own[:poles])
    settled_entry = jnp.where(later, back_entry, ahead_entry)
    open_entry = jnp.where(later, ahead_entry, back_entry)
    shift = jnp.exp(-rates * (rows * jnp.where(later, place, reach - 1 - place)).astype(F32))
    sent, settled_entry, open_entry, shift = lax.optimization_barrier(
        (sent, settled_entry, open_entry, shift)
    )
    other = lax.ppermute(sent, "ctx", [(i, i ^ reach) for i in range(blocks)])
    *outs, gate_a, gate_b = pl.pallas_call(
        functools.partial(settled_kernel, seg_len, blocks),
        out_shape=[gate] * 6,
        in_specs=[HBM] * 4 + [VMEM] * (6),
        out_specs=[HBM] * 4 + [VMEM] * 2,
        scratch_shapes=[pltpu.VMEM((rows, channels), BF16)] * 4
        + [dma((2,)), dma((2,)), dma((count, 2))],
        compiler_params=limit,
        cost_estimate=pl.CostEstimate(
            flops=work * 2, bytes_accessed=rows * channels * 12, transcendentals=0
        ),
        name="settled",
    )(*arrays, ends, starts, table, settled_entry, *found)
    entry = open_entry + shift * other
    first = 8
    return pl.pallas_call(
        functools.partial(last_kernel, seg_len, blocks),
        out_shape=[gate] * 4,
        in_specs=[VMEM] * first + [HBM] * 4,
        out_specs=[HBM] * 4,
        input_output_aliases={first + j: j for j in range(4)},
        scratch_shapes=[pltpu.VMEM((rows, channels), BF16)] * 2 + [dma((count, 2))],
        compiler_params=limit,
        name="last",
    )(gate_a, gate_b, ends, starts, table, entry, *found, *outs)


def solution(mesh):
    spread = P(("groups", "ctx"), None)
    return jax.shard_map(
        shards,
        mesh=mesh,
        in_specs=(spread,) * 4 + (P(),) * 3,
        out_specs=(spread,) * 4,
        check_vma=False,
    )
```

```python
import functools
import jax
import jax.numpy as jnp
from jax import lax
from jax.experimental import pallas as pl
from jax.experimental.pallas import tpu as pltpu
from jax.sharding import PartitionSpec as P

SEGS = 8
LANES = 128
PAD = 8
STEP = 16
CHUNK = 16
F32 = jnp.float32
BF16 = jnp.bfloat16
VMEM = pl.BlockSpec(memory_space=pltpu.VMEM)
HBM = pl.BlockSpec(memory_space=pltpu.HBM)


def lane_slice(half):
    return slice(half * LANES, (half + 1) * LANES)


def add_up(terms):
    while len(terms) > 1:
        odd = [terms[-1]] if len(terms) % 2 else []
        terms = [a + b for a, b in zip(terms[::2], terms[1::2])] + odd
    return terms[0]


def spread_rows(table, lanes, count):
    return [jnp.broadcast_to(table[k : k + 1, lanes], (8, LANES)) for k in range(count)]


def factor_tables(rates, rows, blocks, factor_ref):
    poles, channels = rates.shape
    me = lax.axis_index("ctx")
    one = jnp.ones((poles, channels), F32)
    zero = jnp.zeros((poles, channels), F32)
    base = 0
    for bit in range(blocks.bit_length() - 1):
        reach = 1 << bit
        later = jnp.bitwise_and(jnp.right_shift(me, bit), 1) == 1
        place = jnp.bitwise_and(me, reach - 1)
        gap = jnp.where(later, place, reach - 1 - place).astype(F32)
        shift = jnp.exp(-rates * (float(rows) * gap))
        if 2 * reach < blocks:
            span = jnp.exp(-float(rows * reach) * rates)
            first, second = jnp.where(later, one, span), jnp.where(later, span, one)
            parts = (first, second, second, first)
            parts += (jnp.where(later, shift, zero), jnp.where(later, zero, shift))
        else:
            parts = (shift, jnp.where(later, one, zero))
        for part in parts:
            factor_ref[base : base + poles, :] = part
            base += poles


def state_kernel(
    seg_len,
    blocks,
    outer_hbm,
    inner_hbm,
    values_hbm,
    cotangent_hbm,
    rate_hbm,
    residue_hbm,
    mixed_ref,
    grad_ref,
    gain_ref,
    loss_ref,
    ends_ref,
    starts_ref,
    own_ref,
    table_ref,
    factor_ref,
    outer_ref,
    inner_ref,
    values_ref,
    cotangent_ref,
    copy_sems,
    table_sems,
):
    poles = rate_hbm.shape[0]
    pitch = seg_len + PAD
    count = mixed_ref.shape[0]
    chunks = seg_len // CHUNK
    tables = [
        pltpu.make_async_copy(
            source, table_ref.at[pl.ds(j * poles, poles), :], table_sems.at[j]
        )
        for j, source in enumerate((rate_hbm, residue_hbm))
    ]
    for copy in tables:
        copy.start()
    pairs = (
        (inner_hbm, inner_ref),
        (values_hbm, values_ref),
        (outer_hbm, outer_ref),
        (cotangent_hbm, cotangent_ref),
    )
    copies = []
    for h in range(count):
        line = []
        for j, (source, target) in enumerate(pairs):
            copy = pltpu.make_async_copy(
                source.at[:, lane_slice(h)], target.at[:, lane_slice(h)], copy_sems.at[h, j]
            )
            copy.start()
            line.append(copy)
        copies.append(line)
    for copy in tables:
        copy.wait()
    rate_table = table_ref[0:poles, :]
    decay = jnp.exp(-rate_table)
    chunk_decay = jnp.exp(-float(CHUNK) * rate_table)
    seg_decay = jnp.exp(-float(seg_len) * rate_table)
    factor_tables(rate_table, seg_len * SEGS, blocks, factor_ref)
    for h in range(count):
        lanes = lane_slice(h)
        for copy in copies[h]:
            copy.wait()

        def convert(q, _):
            source = pl.ds(pl.multiple_of(q * seg_len, 16), seg_len)
            target = pl.ds(pl.multiple_of(q * pitch, 8), seg_len)
            mixed = inner_ref[source, lanes].astype(F32) * values_ref[source, lanes].astype(F32)
            mixed_ref[h, target, :] = mixed.astype(BF16).astype(F32)
            outer, cotangent = outer_ref[source, lanes], cotangent_ref[source, lanes]
            grad_ref[h, target, :] = outer.astype(F32) * cotangent.astype(F32)
            return _

        lax.fori_loop(0, SEGS, convert, 0)
        steps = spread_rows(decay, lanes, poles)

        def body(m, _):
            base = m * CHUNK
            for j in range(CHUNK):
                x = mixed_ref[h, pl.ds(base + j, SEGS, stride=pitch), :]
                g = grad_ref[h, pl.ds(base + CHUNK - 1 - j, SEGS, stride=pitch), :]
                if j:
                    ahead = [steps[k] * ahead[k] + x for k in range(poles)]
                    back = [steps[k] * back[k] + g for k in range(poles)]
                else:
                    ahead, back = [x] * poles, [g] * poles
            for k in range(poles):
                rows = pl.ds(pl.multiple_of((m * poles + k) * SEGS, SEGS), SEGS)
                gain_ref[h, rows, :] = ahead[k]
                loss_ref[h, rows, :] = back[k]
            return _

        lax.fori_loop(0, chunks, body, 0)
        longer = spread_rows(chunk_decay, lanes, poles)
        for k in range(poles):
            ahead = gain_ref[h, SEGS * k : SEGS * (k + 1), :]
            last = ((chunks - 1) * poles + k) * SEGS
            back = loss_ref[h, last : last + SEGS, :]
            for m in range(1, chunks):
                row = (m * poles + k) * SEGS
                ahead = longer[k] * ahead + gain_ref[h, row : row + SEGS, :]
                row = ((chunks - 1 - m) * poles + k) * SEGS
                back = longer[k] * back + loss_ref[h, row : row + SEGS, :]
            ends_ref[h, SEGS * k : SEGS * (k + 1), :] = ahead
            starts_ref[h, SEGS * k : SEGS * (k + 1), :] = back
        ahead = jnp.zeros((poles, LANES), F32)
        back = jnp.zeros((poles, LANES), F32)
        for q in range(SEGS):
            ahead = seg_decay[:, lanes] * ahead + ends_ref[h, pl.ds(q, poles, stride=SEGS), :]
            back = seg_decay[:, lanes] * back + starts_ref[
                h, pl.ds(SEGS - 1 - q, poles, stride=SEGS), :
            ]
        own_ref[0:poles, lanes] = ahead
        own_ref[poles : 2 * poles, lanes] = back


def local_kernel(seg_len, backward, signal_ref, table_ref, skip_ref, out_ref):
    poles = table_ref.shape[0] // 2
    pitch = seg_len + PAD
    chunks = seg_len // CHUNK
    weight = table_ref[poles : 2 * poles, :]
    decay = jnp.exp(-table_ref[0:poles, :])
    rows = []
    for lag in range(CHUNK):
        rows.append(jnp.sum(weight, axis=0, keepdims=True))
        weight = weight * decay
    rows[0] = rows[0] + skip_ref[...]
    for h in range(signal_ref.shape[0]):
        lanes = lane_slice(h)
        taps = [jnp.broadcast_to(row[:, lanes], (SEGS, LANES)) for row in rows]

        def fetch(m):
            return tuple(
                signal_ref[h, pl.ds(m * CHUNK + j, SEGS, stride=pitch), :] for j in range(CHUNK)
            )

        def body(m, held):
            following = fetch(jnp.minimum(m + 1, chunks - 1))
            for j in range(CHUNK):
                lags = range(CHUNK - j) if backward else range(j + 1)
                terms = [taps[lag] * held[j + lag if backward else j - lag] for lag in lags]
                out_ref[h, pl.ds(m * CHUNK + j, SEGS, stride=pitch), :] = add_up(terms)
            return following

        lax.fori_loop(0, chunks, body, fetch(0))


def finish_way(
    seg_len,
    backward,
    gates,
    local_ref,
    chunk_ref,
    edge_ref,
    table_ref,
    entry_ref,
    targets,
    state_ref,
    total_ref,
    sems,
):
    poles = table_ref.shape[0] // 2
    pitch = seg_len + PAD
    chunks = seg_len // CHUNK
    rates = table_ref[0:poles, :]
    decay = jnp.exp(-rates)
    seg_decay = jnp.exp(-float(seg_len) * rates)
    loads = [copy for copy, _ in gates]
    gate_refs = [ref for _, ref in gates]
    copies = []
    for h in range(local_ref.shape[0]):
        lanes = lane_slice(h)
        state = entry_ref[:, lanes]
        for n in range(SEGS):
            q = SEGS - 1 - n if backward else n
            state_ref[pl.ds(q, poles, stride=SEGS), :] = state
            if n < SEGS - 1:
                edge = edge_ref[h, pl.ds(q, poles, stride=SEGS), :]
                state = seg_decay[:, lanes] * state + edge
        steps = spread_rows(decay, lanes, poles)
        weights = spread_rows(table_ref[poles : 2 * poles, :], lanes, poles)
        carried = tuple(
            weights[k] * state_ref[SEGS * k : SEGS * (k + 1), :] for k in range(poles)
        )

        def body(n, carried):
            m = chunks - 1 - n if backward else n
            for i in range(CHUNK):
                row = pl.ds(m * CHUNK + (CHUNK - 1 - i if backward else i), SEGS, stride=pitch)
                carried = [steps[k] * carried[k] for k in range(poles)]
                total_ref[row, :] = add_up([*carried, local_ref[h, row, :]])
            return tuple(
                carried[k]
                + weights[k]
                * chunk_ref[h, pl.ds(pl.multiple_of((m * poles + k) * SEGS, SEGS), SEGS), :]
                for k in range(poles)
            )

        lax.fori_loop(0, chunks, body, carried)
        for copy in loads:
            copy.wait()
        loads = []

        def gate(q, _):
            whole = total_ref[pl.ds(pl.multiple_of(q * pitch, 8), seg_len), :]
            rows = pl.ds(pl.multiple_of(q * seg_len, STEP), seg_len)
            for gate_ref, (target, _hbm) in zip(gate_refs, targets):
                target[rows, lanes] = (gate_ref[rows, lanes].astype(F32) * whole).astype(BF16)
            return _

        lax.fori_loop(0, SEGS, gate, 0)
        for j, (target, hbm) in enumerate(targets):
            copy = pltpu.make_async_copy(target.at[:, lanes], hbm.at[:, lanes], sems.at[h, j])
            copy.start()
            copies.append(copy)
    for copy in copies:
        copy.wait()


def finish_kernel(
    seg_len,
    blocks,
    settled,
    outer_hbm,
    inner_hbm,
    values_hbm,
    cotangent_hbm,
    ahead_ref,
    back_ref,
    gain_ref,
    loss_ref,
    ends_ref,
    starts_ref,
    table_ref,
    entry_ref,
    *rest,
):
    outs, (gate_a, gate_b, out_a, out_b, state_ref, total_ref, load_sems, out_sems) = (
        rest[-12:-8],
        rest[-8:],
    )
    layer_hbm, outer_grad_hbm, inner_grad_hbm, values_grad_hbm = outs
    later = lax.axis_index("ctx") >= blocks // 2

    def run(backward):
        if backward:
            sources = (values_hbm, inner_hbm)
            targets = ((out_a, inner_grad_hbm), (out_b, values_grad_hbm))
            parts = (back_ref, loss_ref, starts_ref)
        else:
            sources = (outer_hbm, cotangent_hbm)
            targets = ((out_a, layer_hbm), (out_b, outer_grad_hbm))
            parts = (ahead_ref, gain_ref, ends_ref)
        gates = []
        for j, (source, target) in enumerate(zip(sources, (gate_a, gate_b))):
            copy = pltpu.make_async_copy(source, target, load_sems.at[j])
            copy.start()
            gates.append((copy, target))
        finish_way(
            seg_len,
            backward,
            gates,
            *parts,
            table_ref,
            entry_ref,
            targets,
            state_ref,
            total_ref,
            out_sems,
        )

    pl.when(later)(functools.partial(run, settled))
    pl.when(jnp.logical_not(later))(functools.partial(run, not settled))


def shards(outer_gate, inner_gate, values, cotangent, residue, decay_rate, skip_gain):
    rows, channels = values.shape
    poles = residue.shape[1]
    seg_len = rows // SEGS
    padded = SEGS * (seg_len + PAD)
    count = channels // LANES
    blocks = lax.axis_size("ctx")
    levels = blocks.bit_length() - 1
    gate = jax.ShapeDtypeStruct((rows, channels), BF16)
    limit = pltpu.CompilerParams(vmem_limit_bytes=4 << 20)
    work = rows * channels * poles
    dma = pltpu.SemaphoreType.DMA

    def in_hbm(x):
        return pltpu.with_memory_space_constraint(x, pltpu.HBM)

    arrays = [in_hbm(x) for x in (outer_gate, inner_gate, values, cotangent)]
    mixed, grad, gain, loss, ends, starts, own, table, factors = pl.pallas_call(
        functools.partial(state_kernel, seg_len, blocks),
        out_shape=[jax.ShapeDtypeStruct((count, padded, LANES), F32)] * 2
        + [jax.ShapeDtypeStruct((count, rows // CHUNK * poles, LANES), F32)] * 2
        + [jax.ShapeDtypeStruct((count, SEGS * poles, LANES), F32)] * 2
        + [jax.ShapeDtypeStruct((2 * poles, channels), F32)] * 2
        + [jax.ShapeDtypeStruct(((6 * levels - 4) * poles, channels), F32)],
        in_specs=[HBM] * 6,
        out_specs=[VMEM] * 9,
        scratch_shapes=[pltpu.VMEM((rows, channels), BF16)] * 4 + [dma((count, 4)), dma((2,))],
        compiler_params=limit,
        name="states",
    )(*arrays, in_hbm(decay_rate.T), in_hbm(residue.T))
    skip = skip_gain[None, :]

    def local(signal, backward, held):
        signal, _ = lax.optimization_barrier((signal, held))
        return pl.pallas_call(
            functools.partial(local_kernel, seg_len, backward),
            out_shape=jax.ShapeDtypeStruct(signal.shape, F32),
            in_specs=[VMEM] * 3,
            out_specs=VMEM,
            input_output_aliases={0: 0},
            compiler_params=limit,
            cost_estimate=pl.CostEstimate(
                flops=rows * channels * 17, bytes_accessed=signal.size * 8, transcendentals=0
            ),
            name="local",
        )(signal, table, skip)

    jobs = [(mixed, False), (grad, True)]
    found = []
    entry = jnp.zeros_like(own)
    for bit in range(levels - 1):
        reach = 1 << bit
        other = lax.ppermute(own, "ctx", [(i, i ^ reach) for i in range(blocks)])
        pieces = [local(*jobs.pop(0), own)] if bit and jobs else []
        keep, take, join = factors[6 * bit * poles : 6 * (bit + 1) * poles].reshape(
            3, 2 * poles, channels
        )
        entry = entry + join * other
        own = keep * own + take * other
        own, entry, pieces = lax.optimization_barrier((own, entry, pieces))
        found += pieces
    found += [local(*job, own) for job in jobs]
    shift, late = factors[6 * (levels - 1) * poles :].reshape(2, poles, channels)

    def choose(when_later, otherwise):
        return late * when_later + (1.0 - late) * otherwise

    ahead, back = own[:poles], own[poles:]
    ahead_entry, back_entry = entry[:poles], entry[poles:]
    sent, settled_entry, open_entry = lax.optimization_barrier(
        (
            choose(back, ahead),
            choose(back_entry, ahead_entry),
            choose(ahead_entry, back_entry),
        )
    )
    other = lax.ppermute(sent, "ctx", [(i, i ^ (blocks // 2)) for i in range(blocks)])

    def finish(settled, entry, before):
        first = 12
        return pl.pallas_call(
            functools.partial(finish_kernel, seg_len, blocks, settled),
            out_shape=[gate] * 4,
            in_specs=[HBM] * 4 + [VMEM] * 8 + [HBM] * len(before),
            out_specs=[HBM] * 4,
            input_output_aliases={first + j: j for j in range(len(before))},
            scratch_shapes=[pltpu.VMEM((rows, channels), BF16)] * 4
            + [pltpu.VMEM((SEGS * poles, LANES), F32), pltpu.VMEM((padded, LANES), F32)]
            + [dma((2,)), dma((count, 2))],
            compiler_params=limit,
            cost_estimate=pl.CostEstimate(
                flops=work * 2, bytes_accessed=rows * channels * 12, transcendentals=0
            ),
            name="settled" if settled else "last",
        )(*arrays, *found, gain, loss, ends, starts, table, entry, *before)

    outs = finish(True, settled_entry, ())
    return finish(False, open_entry + shift * other, outs)


def solution(mesh):
    spread = P(("groups", "ctx"), None)
    return jax.shard_map(
        shards,
        mesh=mesh,
        in_specs=(spread,) * 4 + (P(),) * 3,
        out_specs=(spread,) * 4,
        check_vma=False,
    )
```

```python
import functools
import jax
import jax.numpy as jnp
from jax import lax
from jax.experimental import pallas as pl
from jax.experimental.pallas import tpu as pltpu
from jax.sharding import PartitionSpec as P

SEGS = 8
LANES = 128
PAD = 8
STEP = 16
CHUNK = 16
PIECES = 2
F32 = jnp.float32
BF16 = jnp.bfloat16
VMEM = pl.BlockSpec(memory_space=pltpu.VMEM)
HBM = pl.BlockSpec(memory_space=pltpu.HBM)


def lane_slice(half):
    return slice(half * LANES, (half + 1) * LANES)


def add_up(terms):
    while len(terms) > 1:
        odd = [terms[-1]] if len(terms) % 2 else []
        terms = [a + b for a, b in zip(terms[::2], terms[1::2])] + odd
    return terms[0]


def spread_rows(table, lanes, count):
    return [jnp.broadcast_to(table[k : k + 1, lanes], (8, LANES)) for k in range(count)]


def factor_tables(rates, rows, blocks, factor_ref):
    poles, channels = rates.shape
    me = lax.axis_index("ctx")
    one = jnp.ones((poles, channels), F32)
    zero = jnp.zeros((poles, channels), F32)
    base = 0
    for bit in range(blocks.bit_length() - 1):
        reach = 1 << bit
        later = jnp.bitwise_and(jnp.right_shift(me, bit), 1) == 1
        place = jnp.bitwise_and(me, reach - 1)
        gap = jnp.where(later, place, reach - 1 - place).astype(F32)
        shift = jnp.exp(-rates * (float(rows) * gap))
        if 2 * reach < blocks:
            span = jnp.exp(-float(rows * reach) * rates)
            first, second = jnp.where(later, one, span), jnp.where(later, span, one)
            parts = (first, second, second, first)
            parts += (jnp.where(later, shift, zero), jnp.where(later, zero, shift))
        else:
            parts = (shift, jnp.where(later, one, zero))
        for part in parts:
            factor_ref[base : base + poles, :] = part
            base += poles


def state_kernel(
    seg_len,
    blocks,
    outer_hbm,
    inner_hbm,
    values_hbm,
    cotangent_hbm,
    rate_hbm,
    residue_hbm,
    mixed_ref,
    grad_ref,
    gain_ref,
    loss_ref,
    ends_ref,
    starts_ref,
    own_ref,
    table_ref,
    factor_ref,
    outer_ref,
    inner_ref,
    values_ref,
    cotangent_ref,
    copy_sems,
    table_sems,
):
    poles = rate_hbm.shape[0]
    pitch = seg_len + PAD
    count = mixed_ref.shape[0]
    chunks = seg_len // CHUNK
    tables = [
        pltpu.make_async_copy(
            source, table_ref.at[pl.ds(j * poles, poles), :], table_sems.at[j]
        )
        for j, source in enumerate((rate_hbm, residue_hbm))
    ]
    for copy in tables:
        copy.start()
    pairs = (
        (inner_hbm, inner_ref),
        (values_hbm, values_ref),
        (outer_hbm, outer_ref),
        (cotangent_hbm, cotangent_ref),
    )
    copies = []
    for h in range(count):
        line = []
        for j, (source, target) in enumerate(pairs):
            copy = pltpu.make_async_copy(
                source.at[:, lane_slice(h)], target.at[:, lane_slice(h)], copy_sems.at[h, j]
            )
            copy.start()
            line.append(copy)
        copies.append(line)
    for copy in tables:
        copy.wait()
    rate_table = table_ref[0:poles, :]
    decay = jnp.exp(-rate_table)
    chunk_decay = jnp.exp(-float(CHUNK) * rate_table)
    seg_decay = jnp.exp(-float(seg_len) * rate_table)
    factor_tables(rate_table, seg_len * SEGS, blocks, factor_ref)
    for h in range(count):
        lanes = lane_slice(h)
        steps = spread_rows(decay, lanes, poles)

        def convert(first_ref, second_ref, target_ref, rounded):
            def segment(q, _):
                source = pl.ds(pl.multiple_of(q * seg_len, STEP), seg_len)
                target = pl.ds(pl.multiple_of(q * pitch, 8), seg_len)
                product = first_ref[source, lanes].astype(F32) * second_ref[
                    source, lanes
                ].astype(F32)
                if rounded:
                    product = product.astype(BF16).astype(F32)
                target_ref[h, target, :] = product
                return _

            lax.fori_loop(0, SEGS, segment, 0)

        def sums(signal_ref, chunk_ref, backward):
            def chunk(m, _):
                for j in range(CHUNK):
                    row = m * CHUNK + (CHUNK - 1 - j if backward else j)
                    x = signal_ref[h, pl.ds(row, SEGS, stride=pitch), :]
                    state = [steps[k] * state[k] + x for k in range(poles)] if j else [x] * poles
                for k in range(poles):
                    rows = pl.ds(pl.multiple_of((m * poles + k) * SEGS, SEGS), SEGS)
                    chunk_ref[h, rows, :] = state[k]
                return _

            lax.fori_loop(0, chunks, chunk, 0, unroll=2)

        for copy in copies[h][:2]:
            copy.wait()
        convert(inner_ref, values_ref, mixed_ref, True)
        sums(mixed_ref, gain_ref, False)
        for copy in copies[h][2:]:
            copy.wait()
        convert(outer_ref, cotangent_ref, grad_ref, False)
        sums(grad_ref, loss_ref, True)
        longer = spread_rows(chunk_decay, lanes, poles)
        for k in range(poles):
            ahead = gain_ref[h, SEGS * k : SEGS * (k + 1), :]
            last = ((chunks - 1) * poles + k) * SEGS
            back = loss_ref[h, last : last + SEGS, :]
            for m in range(1, chunks):
                row = (m * poles + k) * SEGS
                ahead = longer[k] * ahead + gain_ref[h, row : row + SEGS, :]
                row = ((chunks - 1 - m) * poles + k) * SEGS
                back = longer[k] * back + loss_ref[h, row : row + SEGS, :]
            ends_ref[h, SEGS * k : SEGS * (k + 1), :] = ahead
            starts_ref[h, SEGS * k : SEGS * (k + 1), :] = back
        ahead = jnp.zeros((poles, LANES), F32)
        back = jnp.zeros((poles, LANES), F32)
        for q in range(SEGS):
            ahead = seg_decay[:, lanes] * ahead + ends_ref[h, pl.ds(q, poles, stride=SEGS), :]
            back = seg_decay[:, lanes] * back + starts_ref[
                h, pl.ds(SEGS - 1 - q, poles, stride=SEGS), :
            ]
        own_ref[0:poles, lanes] = ahead
        own_ref[poles : 2 * poles, lanes] = back


def local_kernel(seg_len, backward, signal_ref, table_ref, skip_ref, out_ref):
    poles = table_ref.shape[0] // 2
    pitch = seg_len + PAD
    chunks = seg_len // CHUNK
    weight = table_ref[poles : 2 * poles, :]
    decay = jnp.exp(-table_ref[0:poles, :])
    rows = []
    for lag in range(CHUNK):
        rows.append(jnp.sum(weight, axis=0, keepdims=True))
        weight = weight * decay
    rows[0] = rows[0] + skip_ref[...]
    for h in range(signal_ref.shape[0]):
        lanes = lane_slice(h)
        taps = [jnp.broadcast_to(row[:, lanes], (SEGS, LANES)) for row in rows]

        def fetch(m):
            return tuple(
                signal_ref[h, pl.ds(m * CHUNK + j, SEGS, stride=pitch), :] for j in range(CHUNK)
            )

        def body(m, held):
            following = fetch(jnp.minimum(m + 1, chunks - 1))
            for j in range(CHUNK):
                lags = range(CHUNK - j) if backward else range(j + 1)
                terms = [taps[lag] * held[j + lag if backward else j - lag] for lag in lags]
                out_ref[h, pl.ds(m * CHUNK + j, SEGS, stride=pitch), :] = add_up(terms)
            return following

        lax.fori_loop(0, chunks, body, fetch(0))


def finish_way(
    seg_len,
    backward,
    gates,
    local_ref,
    chunk_ref,
    edge_ref,
    table_ref,
    entry_ref,
    targets,
    state_ref,
    total_ref,
    send,
):
    poles = table_ref.shape[0] // 2
    pitch = seg_len + PAD
    chunks = seg_len // CHUNK
    rates = table_ref[0:poles, :]
    decay = jnp.exp(-rates)
    seg_decay = jnp.exp(-float(seg_len) * rates)
    for h in range(local_ref.shape[0]):
        lanes = lane_slice(h)
        state = entry_ref[:, lanes]
        for n in range(SEGS):
            q = SEGS - 1 - n if backward else n
            state_ref[pl.ds(q, poles, stride=SEGS), :] = state
            if n < SEGS - 1:
                edge = edge_ref[h, pl.ds(q, poles, stride=SEGS), :]
                state = seg_decay[:, lanes] * state + edge
        steps = spread_rows(decay, lanes, poles)
        weights = spread_rows(table_ref[poles : 2 * poles, :], lanes, poles)
        carried = tuple(
            weights[k] * state_ref[SEGS * k : SEGS * (k + 1), :] for k in range(poles)
        )

        def body(n, carried):
            m = chunks - 1 - n if backward else n
            for i in range(CHUNK):
                row = pl.ds(m * CHUNK + (CHUNK - 1 - i if backward else i), SEGS, stride=pitch)
                carried = [steps[k] * carried[k] for k in range(poles)]
                total_ref[row, :] = add_up([*carried, local_ref[h, row, :]])
            return tuple(
                carried[k]
                + weights[k]
                * chunk_ref[h, pl.ds(pl.multiple_of((m * poles + k) * SEGS, SEGS), SEGS), :]
                for k in range(poles)
            )

        lax.fori_loop(0, chunks, body, carried)

        def gate(q, _):
            whole = total_ref[pl.ds(pl.multiple_of(q * pitch, 8), seg_len), :]
            rows = pl.ds(pl.multiple_of(q * seg_len, STEP), seg_len)
            for gate_ref, target in zip(gates, targets):
                target[rows, lanes] = (gate_ref[rows, lanes].astype(F32) * whole).astype(BF16)
            return _

        for part in range(PIECES):
            first, last = part * SEGS // PIECES, (part + 1) * SEGS // PIECES
            lax.fori_loop(first, last, gate, 0)
            send(h, part, pl.ds(first * seg_len, (last - first) * seg_len), lanes)


def finish_kernel(
    seg_len,
    blocks,
    settled,
    outer_ref,
    inner_ref,
    values_ref,
    cotangent_ref,
    ahead_ref,
    back_ref,
    gain_ref,
    loss_ref,
    ends_ref,
    starts_ref,
    table_ref,
    entry_ref,
    *rest,
):
    if settled:
        out_a, out_b, state_ref, total_ref = rest
    else:
        done_a, done_b, *outs, out_a, out_b, state_ref, total_ref, done_sems, out_sems = rest
    later = lax.axis_index("ctx") >= blocks // 2

    def run(backward):
        copies = []
        if not settled:
            here = (2, 3) if backward else (0, 1)
            there = (0, 1) if backward else (2, 3)
            for j, ready in enumerate((done_a, done_b)):
                copy = pltpu.make_async_copy(ready, outs[there[j]], done_sems.at[j])
                copy.start()
                copies.append(copy)

        def send(h, part, rows, lanes):
            if settled:
                return
            for j, ready in enumerate((out_a, out_b)):
                copy = pltpu.make_async_copy(
                    ready.at[rows, lanes], outs[here[j]].at[rows, lanes], out_sems.at[h, part, j]
                )
                copy.start()
                copies.append(copy)

        if backward:
            gates = (values_ref, inner_ref)
            parts = (back_ref, loss_ref, starts_ref)
        else:
            gates = (outer_ref, cotangent_ref)
            parts = (ahead_ref, gain_ref, ends_ref)
        finish_way(
            seg_len,
            backward,
            gates,
            *parts,
            table_ref,
            entry_ref,
            (out_a, out_b),
            state_ref,
            total_ref,
            send,
        )
        for copy in copies:
            copy.wait()

    pl.when(later)(functools.partial(run, settled))
    pl.when(jnp.logical_not(later))(functools.partial(run, not settled))


def shards(outer_gate, inner_gate, values, cotangent, residue, decay_rate, skip_gain):
    rows, channels = values.shape
    poles = residue.shape[1]
    seg_len = rows // SEGS
    padded = SEGS * (seg_len + PAD)
    count = channels // LANES
    blocks = lax.axis_size("ctx")
    levels = blocks.bit_length() - 1
    gate = jax.ShapeDtypeStruct((rows, channels), BF16)
    limit = pltpu.CompilerParams(vmem_limit_bytes=4 << 20)
    work = rows * channels * poles
    dma = pltpu.SemaphoreType.DMA

    def in_hbm(x):
        return pltpu.with_memory_space_constraint(x, pltpu.HBM)

    arrays = [in_hbm(x) for x in (outer_gate, inner_gate, values, cotangent)]
    mixed, grad, gain, loss, ends, starts, own, table, factors, *gates = pl.pallas_call(
        functools.partial(state_kernel, seg_len, blocks),
        out_shape=[jax.ShapeDtypeStruct((count, padded, LANES), F32)] * 2
        + [jax.ShapeDtypeStruct((count, rows // CHUNK * poles, LANES), F32)] * 2
        + [jax.ShapeDtypeStruct((count, SEGS * poles, LANES), F32)] * 2
        + [jax.ShapeDtypeStruct((2 * poles, channels), F32)] * 2
        + [jax.ShapeDtypeStruct(((6 * levels - 4) * poles, channels), F32)]
        + [gate] * 4,
        in_specs=[HBM] * 6,
        out_specs=[VMEM] * 13,
        scratch_shapes=[dma((count, 4)), dma((2,))],
        compiler_params=limit,
        name="states",
    )(*arrays, in_hbm(decay_rate.T), in_hbm(residue.T))
    skip = skip_gain[None, :]

    def local(signal, backward, held):
        signal, _ = lax.optimization_barrier((signal, held))
        return pl.pallas_call(
            functools.partial(local_kernel, seg_len, backward),
            out_shape=jax.ShapeDtypeStruct(signal.shape, F32),
            in_specs=[VMEM] * 3,
            out_specs=VMEM,
            input_output_aliases={0: 0},
            compiler_params=limit,
            cost_estimate=pl.CostEstimate(
                flops=rows * channels * 17, bytes_accessed=signal.size * 8, transcendentals=0
            ),
            name="local",
        )(signal, table, skip)

    def partners(bit):
        return [(i, i ^ (1 << bit) ^ (1 if bit else 0)) for i in range(blocks)]

    jobs = [(mixed, False), (grad, True)]
    found = []
    entry = jnp.zeros_like(own)
    for bit in range(levels - 1):
        other = lax.ppermute(own, "ctx", partners(bit))
        pieces = [local(*jobs.pop(0), own)] if bit and jobs else []
        keep, take, join = factors[6 * bit * poles : 6 * (bit + 1) * poles].reshape(
            3, 2 * poles, channels
        )
        entry = entry + join * other
        own = keep * own + take * other
        own, entry, pieces = lax.optimization_barrier((own, entry, pieces))
        found += pieces
    found += [local(*job, own) for job in jobs]
    shift, late = factors[6 * (levels - 1) * poles :].reshape(2, poles, channels)

    def choose(when_later, otherwise):
        return late * when_later + (1.0 - late) * otherwise

    ahead, back = own[:poles], own[poles:]
    ahead_entry, back_entry = entry[:poles], entry[poles:]
    sent, settled_entry, open_entry = lax.optimization_barrier(
        (
            choose(back, ahead),
            choose(back_entry, ahead_entry),
            choose(ahead_entry, back_entry),
        )
    )
    other = lax.ppermute(sent, "ctx", partners(levels - 1))

    def finish(settled, entry, before):
        work_space = [pltpu.VMEM((SEGS * poles, LANES), F32), pltpu.VMEM((padded, LANES), F32)]
        if not settled:
            work_space = [pltpu.VMEM((rows, channels), BF16)] * 2 + work_space
            work_space += [dma((2,)), dma((count, PIECES, 2))]
        return pl.pallas_call(
            functools.partial(finish_kernel, seg_len, blocks, settled),
            out_shape=[gate] * (2 if settled else 4),
            in_specs=[VMEM] * (12 + len(before)),
            out_specs=[VMEM] * 2 if settled else [HBM] * 4,
            scratch_shapes=work_space,
            compiler_params=limit,
            cost_estimate=pl.CostEstimate(
                flops=work * 2, bytes_accessed=rows * channels * 12, transcendentals=0
            ),
            name="settled" if settled else "last",
        )(*gates, *found, gain, loss, ends, starts, table, entry, *before)

    ready = finish(True, settled_entry, ())
    other, ready = lax.optimization_barrier((other, ready))
    return finish(False, open_entry + shift * other, ready)


def solution(mesh):
    spread = P(("groups", "ctx"), None)
    return jax.shard_map(
        shards,
        mesh=mesh,
        in_specs=(spread,) * 4 + (P(),) * 3,
        out_specs=(spread,) * 4,
        check_vma=False,
    )
```

```python
import functools
import jax
import jax.numpy as jnp
from jax import lax
from jax.experimental import pallas as pl
from jax.experimental.pallas import tpu as pltpu
from jax.sharding import PartitionSpec as P

SEGS = 8
LANES = 128
PAD = 8
STEP = 16
CHUNK = 16
PIECES = 2
F32 = jnp.float32
BF16 = jnp.bfloat16
VMEM = pl.BlockSpec(memory_space=pltpu.VMEM)
HBM = pl.BlockSpec(memory_space=pltpu.HBM)


def lane_slice(half):
    return slice(half * LANES, (half + 1) * LANES)


def add_up(terms):
    while len(terms) > 1:
        odd = [terms[-1]] if len(terms) % 2 else []
        terms = [a + b for a, b in zip(terms[::2], terms[1::2])] + odd
    return terms[0]


def spread_rows(table, lanes, count):
    return [jnp.broadcast_to(table[k : k + 1, lanes], (8, LANES)) for k in range(count)]


def factor_tables(rates, rows, blocks, bits, factor_ref):
    poles, channels = rates.shape
    me = lax.axis_index("ctx")
    one = jnp.ones((poles, channels), F32)
    zero = jnp.zeros((poles, channels), F32)
    base = 0
    for bit in bits:
        reach = 1 << bit
        later = jnp.bitwise_and(jnp.right_shift(me, bit), 1) == 1
        place = jnp.bitwise_and(me, reach - 1)
        gap = jnp.where(later, place, reach - 1 - place).astype(F32)
        shift = jnp.exp(-rates * (float(rows) * gap))
        if 2 * reach < blocks:
            span = jnp.exp(-float(rows * reach) * rates)
            first, second = jnp.where(later, one, span), jnp.where(later, span, one)
            parts = (first, second, second, first)
            parts += (jnp.where(later, shift, zero), jnp.where(later, zero, shift))
        else:
            parts = (shift, jnp.where(later, one, zero))
        for part in parts:
            factor_ref[base : base + poles, :] = part
            base += poles


def state_kernel(
    seg_len,
    blocks,
    outer_hbm,
    inner_hbm,
    values_hbm,
    cotangent_hbm,
    rate_hbm,
    residue_hbm,
    mixed_ref,
    grad_ref,
    gain_ref,
    loss_ref,
    ends_ref,
    starts_ref,
    own_ref,
    table_ref,
    factor_ref,
    outer_ref,
    inner_ref,
    values_ref,
    cotangent_ref,
    copy_sems,
    table_sems,
):
    poles = rate_hbm.shape[0]
    pitch = seg_len + PAD
    count = mixed_ref.shape[0]
    chunks = seg_len // CHUNK
    pairs = (
        (inner_hbm, inner_ref),
        (values_hbm, values_ref),
        (outer_hbm, outer_ref),
        (cotangent_hbm, cotangent_ref),
    )
    copies = [
        [
            pltpu.make_async_copy(
                source.at[:, lane_slice(h)], target.at[:, lane_slice(h)], copy_sems.at[h, j]
            )
            for j, (source, target) in enumerate(pairs)
        ]
        for h in range(count)
    ]
    tables = [
        pltpu.make_async_copy(
            source, table_ref.at[pl.ds(j * poles, poles), :], table_sems.at[j]
        )
        for j, source in enumerate((rate_hbm, residue_hbm))
    ]
    first = copies[0][:2]
    for copy in first + tables + copies[0][2:]:
        copy.start()
    for h in range(count):
        lanes = lane_slice(h)

        def convert(first_ref, second_ref, target_ref, rounded):
            def segment(q, _):
                source = pl.ds(pl.multiple_of(q * seg_len, STEP), seg_len)
                target = pl.ds(pl.multiple_of(q * pitch, 8), seg_len)
                first, second = first_ref[source, lanes], second_ref[source, lanes]
                if rounded:
                    product = (first * second).astype(F32)
                else:
                    product = first.astype(F32) * second.astype(F32)
                target_ref[h, target, :] = product
                return _

            lax.fori_loop(0, SEGS, segment, 0, unroll=4)

        def sums(signal_ref, chunk_ref, backward):
            steps = spread_rows(decay, lanes, poles)

            def chunk(m, _):
                for j in range(CHUNK):
                    row = m * CHUNK + (CHUNK - 1 - j if backward else j)
                    x = signal_ref[h, pl.ds(row, SEGS, stride=pitch), :]
                    state = [steps[k] * state[k] + x for k in range(poles)] if j else [x] * poles
                for k in range(poles):
                    rows = pl.ds(pl.multiple_of((m * poles + k) * SEGS, SEGS), SEGS)
                    chunk_ref[h, rows, :] = state[k]
                return _

            lax.fori_loop(0, chunks, chunk, 0, unroll=8)

        for copy in copies[h][:2]:
            copy.wait()
        if h == 0:
            for line in copies[1:]:
                for copy in line:
                    copy.start()
        convert(inner_ref, values_ref, mixed_ref, True)
        if h == 0:
            for copy in tables:
                copy.wait()
            rate_table = table_ref[0:poles, :]
            decay = jnp.exp(-rate_table)
            chunk_decay = jnp.exp(-float(CHUNK) * rate_table)
            seg_decay = jnp.exp(-float(seg_len) * rate_table)
            factor_tables(rate_table, seg_len * SEGS, blocks, range(1), factor_ref)
        sums(mixed_ref, gain_ref, False)
        for copy in copies[h][2:]:
            copy.wait()
        convert(outer_ref, cotangent_ref, grad_ref, False)
        sums(grad_ref, loss_ref, True)
        longer = spread_rows(chunk_decay, lanes, poles)
        for k in range(poles):
            ahead = gain_ref[h, SEGS * k : SEGS * (k + 1), :]
            last = ((chunks - 1) * poles + k) * SEGS
            back = loss_ref[h, last : last + SEGS, :]
            for m in range(1, chunks):
                row = (m * poles + k) * SEGS
                ahead = longer[k] * ahead + gain_ref[h, row : row + SEGS, :]
                row = ((chunks - 1 - m) * poles + k) * SEGS
                back = longer[k] * back + loss_ref[h, row : row + SEGS, :]
            ends_ref[h, SEGS * k : SEGS * (k + 1), :] = ahead
            starts_ref[h, SEGS * k : SEGS * (k + 1), :] = back
        ahead = jnp.zeros((poles, LANES), F32)
        back = jnp.zeros((poles, LANES), F32)
        for q in range(SEGS):
            ahead = seg_decay[:, lanes] * ahead + ends_ref[h, pl.ds(q, poles, stride=SEGS), :]
            back = seg_decay[:, lanes] * back + starts_ref[
                h, pl.ds(SEGS - 1 - q, poles, stride=SEGS), :
            ]
        own_ref[0:poles, lanes] = ahead
        own_ref[poles : 2 * poles, lanes] = back


def local_kernel(seg_len, blocks, backward, signal_ref, table_ref, skip_ref, out_ref, *factor_refs):
    poles = table_ref.shape[0] // 2
    pitch = seg_len + PAD
    chunks = seg_len // CHUNK
    for factor_ref in factor_refs:
        bits = range(1, blocks.bit_length() - 1)
        factor_tables(table_ref[0:poles, :], seg_len * SEGS, blocks, bits, factor_ref)
    weight = table_ref[poles : 2 * poles, :]
    decay = jnp.exp(-table_ref[0:poles, :])
    rows = []
    for lag in range(CHUNK):
        rows.append(jnp.sum(weight, axis=0, keepdims=True))
        weight = weight * decay
    rows[0] = rows[0] + skip_ref[...]
    for h in range(signal_ref.shape[0]):
        lanes = lane_slice(h)
        taps = [jnp.broadcast_to(row[:, lanes], (SEGS, LANES)) for row in rows]

        def fetch(m):
            return tuple(
                signal_ref[h, pl.ds(m * CHUNK + j, SEGS, stride=pitch), :] for j in range(CHUNK)
            )

        def body(m, held):
            following = fetch(jnp.minimum(m + 1, chunks - 1))
            for j in range(CHUNK):
                lags = range(CHUNK - j) if backward else range(j + 1)
                terms = [taps[lag] * held[j + lag if backward else j - lag] for lag in lags]
                out_ref[h, pl.ds(m * CHUNK + j, SEGS, stride=pitch), :] = add_up(terms)
            return following

        lax.fori_loop(0, chunks, body, fetch(0))


def finish_way(
    seg_len,
    backward,
    gates,
    local_ref,
    chunk_ref,
    edge_ref,
    table_ref,
    entry_ref,
    targets,
    state_ref,
    total_ref,
    send,
):
    poles = table_ref.shape[0] // 2
    pitch = seg_len + PAD
    chunks = seg_len // CHUNK
    rates = table_ref[0:poles, :]
    decay = jnp.exp(-rates)
    seg_decay = jnp.exp(-float(seg_len) * rates)
    for h in range(local_ref.shape[0]):
        lanes = lane_slice(h)
        state = entry_ref[:, lanes]
        for n in range(SEGS):
            q = SEGS - 1 - n if backward else n
            state_ref[pl.ds(q, poles, stride=SEGS), :] = state
            if n < SEGS - 1:
                edge = edge_ref[h, pl.ds(q, poles, stride=SEGS), :]
                state = seg_decay[:, lanes] * state + edge
        steps = spread_rows(decay, lanes, poles)
        weights = spread_rows(table_ref[poles : 2 * poles, :], lanes, poles)
        carried = tuple(
            weights[k] * state_ref[SEGS * k : SEGS * (k + 1), :] for k in range(poles)
        )

        def body(n, carried):
            m = chunks - 1 - n if backward else n
            for i in range(CHUNK):
                row = pl.ds(m * CHUNK + (CHUNK - 1 - i if backward else i), SEGS, stride=pitch)
                carried = [steps[k] * carried[k] for k in range(poles)]
                total_ref[row, :] = add_up([*carried, local_ref[h, row, :]])
            return tuple(
                carried[k]
                + weights[k]
                * chunk_ref[h, pl.ds(pl.multiple_of((m * poles + k) * SEGS, SEGS), SEGS), :]
                for k in range(poles)
            )

        lax.fori_loop(0, chunks, body, carried)

        def gate(q, _):
            whole = total_ref[pl.ds(pl.multiple_of(q * pitch, 8), seg_len), :]
            rows = pl.ds(pl.multiple_of(q * seg_len, STEP), seg_len)
            for gate_ref, target in zip(gates, targets):
                target[rows, lanes] = (gate_ref[rows, lanes].astype(F32) * whole).astype(BF16)
            return _

        for part in range(PIECES):
            first, last = part * SEGS // PIECES, (part + 1) * SEGS // PIECES
            lax.fori_loop(first, last, gate, 0, unroll=4)
            send(h, part, pl.ds(first * seg_len, (last - first) * seg_len), lanes)


def finish_kernel(
    seg_len,
    blocks,
    settled,
    outer_ref,
    inner_ref,
    values_ref,
    cotangent_ref,
    ahead_ref,
    back_ref,
    gain_ref,
    loss_ref,
    ends_ref,
    starts_ref,
    table_ref,
    entry_ref,
    *rest,
):
    if settled:
        out_a, out_b, state_ref, total_ref = rest
    else:
        done_a, done_b, *outs, out_a, out_b, state_ref, total_ref, done_sems, out_sems = rest
    later = lax.axis_index("ctx") >= blocks // 2

    def run(backward):
        copies = []
        if not settled:
            here = (2, 3) if backward else (0, 1)
            there = (0, 1) if backward else (2, 3)
            for j, ready in enumerate((done_a, done_b)):
                copy = pltpu.make_async_copy(ready, outs[there[j]], done_sems.at[j])
                copy.start()
                copies.append(copy)

        def send(h, part, rows, lanes):
            if settled:
                return
            for j, ready in enumerate((out_a, out_b)):
                copy = pltpu.make_async_copy(
                    ready.at[rows, lanes], outs[here[j]].at[rows, lanes], out_sems.at[h, part, j]
                )
                copy.start()
                copies.append(copy)

        if backward:
            gates = (values_ref, inner_ref)
            parts = (back_ref, loss_ref, starts_ref)
        else:
            gates = (outer_ref, cotangent_ref)
            parts = (ahead_ref, gain_ref, ends_ref)
        finish_way(
            seg_len,
            backward,
            gates,
            *parts,
            table_ref,
            entry_ref,
            (out_a, out_b),
            state_ref,
            total_ref,
            send,
        )
        for copy in copies:
            copy.wait()

    pl.when(later)(functools.partial(run, settled))
    pl.when(jnp.logical_not(later))(functools.partial(run, not settled))


def shards(outer_gate, inner_gate, values, cotangent, residue, decay_rate, skip_gain):
    rows, channels = values.shape
    poles = residue.shape[1]
    seg_len = rows // SEGS
    padded = SEGS * (seg_len + PAD)
    count = channels // LANES
    blocks = lax.axis_size("ctx")
    levels = blocks.bit_length() - 1
    gate = jax.ShapeDtypeStruct((rows, channels), BF16)
    limit = pltpu.CompilerParams(vmem_limit_bytes=4 << 20)
    work = rows * channels * poles
    dma = pltpu.SemaphoreType.DMA

    def in_hbm(x):
        return pltpu.with_memory_space_constraint(x, pltpu.HBM)

    arrays = [in_hbm(x) for x in (outer_gate, inner_gate, values, cotangent)]
    mixed, grad, gain, loss, ends, starts, own, table, factors, *gates = pl.pallas_call(
        functools.partial(state_kernel, seg_len, blocks),
        out_shape=[jax.ShapeDtypeStruct((count, padded, LANES), F32)] * 2
        + [jax.ShapeDtypeStruct((count, rows // CHUNK * poles, LANES), F32)] * 2
        + [jax.ShapeDtypeStruct((count, SEGS * poles, LANES), F32)] * 2
        + [jax.ShapeDtypeStruct((2 * poles, channels), F32)] * 2
        + [jax.ShapeDtypeStruct((6 * poles, channels), F32)]
        + [gate] * 4,
        in_specs=[HBM] * 6,
        out_specs=[VMEM] * 13,
        scratch_shapes=[dma((count, 4)), dma((2,))],
        compiler_params=limit,
        name="states",
    )(*arrays, in_hbm(decay_rate.T), in_hbm(residue.T))
    skip = skip_gain[None, :]

    def local(signal, backward, held):
        signal, _ = lax.optimization_barrier((signal, held))
        shapes = [jax.ShapeDtypeStruct(signal.shape, F32)]
        if not backward:
            shapes.append(jax.ShapeDtypeStruct((6 * (levels - 2) * poles + 2 * poles, channels), F32))
        return pl.pallas_call(
            functools.partial(local_kernel, seg_len, blocks, backward),
            out_shape=shapes,
            in_specs=[VMEM] * 3,
            out_specs=[VMEM] * len(shapes),
            input_output_aliases={0: 0},
            compiler_params=limit,
            cost_estimate=pl.CostEstimate(
                flops=rows * channels * 17, bytes_accessed=signal.size * 8, transcendentals=0
            ),
            name="local",
        )(signal, table, skip)

    def partners(bit):
        return [(i, i ^ (1 << bit) ^ (1 if bit else 0)) for i in range(blocks)]

    jobs = [(mixed, False), (grad, True)]
    found = []
    entry = jnp.zeros_like(own)
    for bit in range(levels - 1):
        other = lax.ppermute(own, "ctx", partners(bit))
        pieces = []
        if bit and jobs:
            piece, *more = local(*jobs.pop(0), own)
            pieces = [piece]
            factors = more[0] if more else factors
        base = 6 * max(bit - 1, 0) * poles
        keep, take, join = factors[base : base + 6 * poles].reshape(3, 2 * poles, channels)
        entry = entry + join * other
        own = keep * own + take * other
        own, entry, pieces = lax.optimization_barrier((own, entry, pieces))
        found += pieces
    for job in jobs:
        piece, *more = local(*job, own)
        found.append(piece)
        factors = more[0] if more else factors
    shift, late = factors[-2 * poles :].reshape(2, poles, channels)

    def choose(when_later, otherwise):
        return late * when_later + (1.0 - late) * otherwise

    ahead, back = own[:poles], own[poles:]
    ahead_entry, back_entry = entry[:poles], entry[poles:]
    sent, settled_entry, open_entry = lax.optimization_barrier(
        (
            choose(back, ahead),
            choose(back_entry, ahead_entry),
            choose(ahead_entry, back_entry),
        )
    )
    other = lax.ppermute(sent, "ctx", partners(levels - 1))

    def finish(settled, entry, before):
        work_space = [pltpu.VMEM((SEGS * poles, LANES), F32), pltpu.VMEM((padded, LANES), F32)]
        if not settled:
            work_space = [pltpu.VMEM((rows, channels), BF16)] * 2 + work_space
            work_space += [dma((2,)), dma((count, PIECES, 2))]
        return pl.pallas_call(
            functools.partial(finish_kernel, seg_len, blocks, settled),
            out_shape=[gate] * (2 if settled else 4),
            in_specs=[VMEM] * (12 + len(before)),
            out_specs=[VMEM] * 2 if settled else [HBM] * 4,
            scratch_shapes=work_space,
            compiler_params=limit,
            cost_estimate=pl.CostEstimate(
                flops=work * 2, bytes_accessed=rows * channels * 12, transcendentals=0
            ),
            name="settled" if settled else "last",
        )(*gates, *found, gain, loss, ends, starts, table, entry, *before)

    ready = finish(True, settled_entry, ())
    other, ready = lax.optimization_barrier((other, ready))
    return finish(False, open_entry + shift * other, ready)


def solution(mesh):
    spread = P(("groups", "ctx"), None)
    return jax.shard_map(
        shards,
        mesh=mesh,
        in_specs=(spread,) * 4 + (P(),) * 3,
        out_specs=(spread,) * 4,
        check_vma=False,
    )
```

```python
import functools
import jax
import jax.numpy as jnp
from jax import lax
from jax.experimental import pallas as pl
from jax.experimental.pallas import tpu as pltpu
from jax.sharding import PartitionSpec as P

SEGS = 8
LANES = 128
PAD = 8
STEP = 16
CHUNK = 16
PIECES = 2
F32 = jnp.float32
BF16 = jnp.bfloat16
VMEM = pl.BlockSpec(memory_space=pltpu.VMEM)
HBM = pl.BlockSpec(memory_space=pltpu.HBM)


def lane_slice(half):
    return slice(half * LANES, (half + 1) * LANES)


def add_up(terms):
    while len(terms) > 1:
        odd = [terms[-1]] if len(terms) % 2 else []
        terms = [a + b for a, b in zip(terms[::2], terms[1::2])] + odd
    return terms[0]


def spread_rows(table, lanes, count):
    return [jnp.broadcast_to(table[k : k + 1, lanes], (8, LANES)) for k in range(count)]


def factor_tables(rates, rows, blocks, bits, factor_ref):
    poles, channels = rates.shape
    me = lax.axis_index("ctx")
    one = jnp.ones((poles, channels), F32)
    zero = jnp.zeros((poles, channels), F32)
    base = 0
    for bit in bits:
        reach = 1 << bit
        later = jnp.bitwise_and(jnp.right_shift(me, bit), 1) == 1
        place = jnp.bitwise_and(me, reach - 1)
        gap = jnp.where(later, place, reach - 1 - place).astype(F32)
        shift = jnp.exp(-rates * (float(rows) * gap))
        if 2 * reach < blocks:
            span = jnp.exp(-float(rows * reach) * rates)
            first, second = jnp.where(later, one, span), jnp.where(later, span, one)
            parts = (first, second, second, first)
            parts += (jnp.where(later, shift, zero), jnp.where(later, zero, shift))
        else:
            parts = (shift, jnp.where(later, one, zero))
        for part in parts:
            factor_ref[base : base + poles, :] = part
            base += poles


def state_kernel(
    seg_len,
    blocks,
    outer_hbm,
    inner_hbm,
    values_hbm,
    cotangent_hbm,
    rate_hbm,
    residue_hbm,
    mixed_ref,
    grad_ref,
    gain_ref,
    loss_ref,
    ends_ref,
    starts_ref,
    own_ref,
    table_ref,
    factor_ref,
    outer_ref,
    inner_ref,
    values_ref,
    cotangent_ref,
    copy_sems,
    table_sems,
):
    poles = rate_hbm.shape[0]
    pitch = seg_len + PAD
    count = mixed_ref.shape[0]
    chunks = seg_len // CHUNK
    pairs = (
        (inner_hbm, inner_ref),
        (values_hbm, values_ref),
        (outer_hbm, outer_ref),
        (cotangent_hbm, cotangent_ref),
    )
    copies = [
        [
            pltpu.make_async_copy(
                source.at[:, lane_slice(h)], target.at[:, lane_slice(h)], copy_sems.at[h, j]
            )
            for j, (source, target) in enumerate(pairs)
        ]
        for h in range(count)
    ]
    tables = [
        pltpu.make_async_copy(
            source, table_ref.at[pl.ds(j * poles, poles), :], table_sems.at[j]
        )
        for j, source in enumerate((rate_hbm, residue_hbm))
    ]
    first = copies[0][:2]
    for copy in first + tables + copies[0][2:]:
        copy.start()
    for h in range(count):
        lanes = lane_slice(h)

        def convert(first_ref, second_ref, target_ref, rounded):
            def segment(q, _):
                source = pl.ds(pl.multiple_of(q * seg_len, STEP), seg_len)
                target = pl.ds(pl.multiple_of(q * pitch, 8), seg_len)
                first, second = first_ref[source, lanes], second_ref[source, lanes]
                if rounded:
                    product = (first * second).astype(F32)
                else:
                    product = first.astype(F32) * second.astype(F32)
                target_ref[h, target, :] = product
                return _

            lax.fori_loop(0, SEGS, segment, 0, unroll=4)

        def sums(signal_ref, chunk_ref, backward):
            steps = spread_rows(decay, lanes, poles)

            def chunk(m, _):
                for j in range(CHUNK):
                    row = m * CHUNK + (CHUNK - 1 - j if backward else j)
                    x = signal_ref[h, pl.ds(row, SEGS, stride=pitch), :]
                    state = [steps[k] * state[k] + x for k in range(poles)] if j else [x] * poles
                for k in range(poles):
                    rows = pl.ds(pl.multiple_of((m * poles + k) * SEGS, SEGS), SEGS)
                    chunk_ref[h, rows, :] = state[k]
                return _

            lax.fori_loop(0, chunks, chunk, 0, unroll=8)

        for copy in copies[h][:2]:
            copy.wait()
        if h == 0:
            for line in copies[1:]:
                for copy in line:
                    copy.start()
        convert(inner_ref, values_ref, mixed_ref, True)
        if h == 0:
            for copy in tables:
                copy.wait()
            rate_table = table_ref[0:poles, :]
            decay = jnp.exp(-rate_table)
            chunk_decay = jnp.exp(-float(CHUNK) * rate_table)
            seg_decay = jnp.exp(-float(seg_len) * rate_table)
            factor_tables(rate_table, seg_len * SEGS, blocks, range(1), factor_ref)
        sums(mixed_ref, gain_ref, False)
        for copy in copies[h][2:]:
            copy.wait()
        convert(outer_ref, cotangent_ref, grad_ref, False)
        sums(grad_ref, loss_ref, True)
        longer = spread_rows(chunk_decay, lanes, poles)
        for k in range(poles):
            ahead = gain_ref[h, SEGS * k : SEGS * (k + 1), :]
            last = ((chunks - 1) * poles + k) * SEGS
            back = loss_ref[h, last : last + SEGS, :]
            for m in range(1, chunks):
                row = (m * poles + k) * SEGS
                ahead = longer[k] * ahead + gain_ref[h, row : row + SEGS, :]
                row = ((chunks - 1 - m) * poles + k) * SEGS
                back = longer[k] * back + loss_ref[h, row : row + SEGS, :]
            ends_ref[h, SEGS * k : SEGS * (k + 1), :] = ahead
            starts_ref[h, SEGS * k : SEGS * (k + 1), :] = back
        ahead = jnp.zeros((poles, LANES), F32)
        back = jnp.zeros((poles, LANES), F32)
        for q in range(SEGS):
            ahead = seg_decay[:, lanes] * ahead + ends_ref[h, pl.ds(q, poles, stride=SEGS), :]
            back = seg_decay[:, lanes] * back + starts_ref[
                h, pl.ds(SEGS - 1 - q, poles, stride=SEGS), :
            ]
        own_ref[0:poles, lanes] = ahead
        own_ref[poles : 2 * poles, lanes] = back


def local_kernel(seg_len, blocks, backward, signal_ref, table_ref, skip_ref, out_ref, *factor_refs):
    poles = table_ref.shape[0] // 2
    pitch = seg_len + PAD
    chunks = seg_len // CHUNK
    for factor_ref in factor_refs:
        bits = range(1, blocks.bit_length() - 1)
        factor_tables(table_ref[0:poles, :], seg_len * SEGS, blocks, bits, factor_ref)
    weight = table_ref[poles : 2 * poles, :]
    decay = jnp.exp(-table_ref[0:poles, :])
    rows = []
    for lag in range(CHUNK):
        rows.append(jnp.sum(weight, axis=0, keepdims=True))
        weight = weight * decay
    rows[0] = rows[0] + skip_ref[...]
    for h in range(signal_ref.shape[0]):
        lanes = lane_slice(h)
        taps = [jnp.broadcast_to(row[:, lanes], (SEGS, LANES)) for row in rows]

        def fetch(m):
            return tuple(
                signal_ref[h, pl.ds(m * CHUNK + j, SEGS, stride=pitch), :] for j in range(CHUNK)
            )

        def body(m, held):
            following = fetch(jnp.minimum(m + 1, chunks - 1))
            for j in range(CHUNK):
                lags = range(CHUNK - j) if backward else range(j + 1)
                terms = [taps[lag] * held[j + lag if backward else j - lag] for lag in lags]
                out_ref[h, pl.ds(m * CHUNK + j, SEGS, stride=pitch), :] = add_up(terms)
            return following

        lax.fori_loop(0, chunks, body, fetch(0))


def finish_way(
    seg_len,
    backward,
    gates,
    local_ref,
    chunk_ref,
    edge_ref,
    table_ref,
    entry,
    targets,
    state_ref,
    total_ref,
    send,
):
    poles = table_ref.shape[0] // 2
    pitch = seg_len + PAD
    chunks = seg_len // CHUNK
    rates = table_ref[0:poles, :]
    decay = jnp.exp(-rates)
    seg_decay = jnp.exp(-float(seg_len) * rates)
    for h in range(local_ref.shape[0]):
        lanes = lane_slice(h)
        state = entry(lanes)
        for n in range(SEGS):
            q = SEGS - 1 - n if backward else n
            state_ref[pl.ds(q, poles, stride=SEGS), :] = state
            if n < SEGS - 1:
                edge = edge_ref[h, pl.ds(q, poles, stride=SEGS), :]
                state = seg_decay[:, lanes] * state + edge
        steps = spread_rows(decay, lanes, poles)
        weights = spread_rows(table_ref[poles : 2 * poles, :], lanes, poles)
        carried = tuple(
            weights[k] * state_ref[SEGS * k : SEGS * (k + 1), :] for k in range(poles)
        )

        def body(n, carried):
            m = chunks - 1 - n if backward else n
            for i in range(CHUNK):
                row = pl.ds(m * CHUNK + (CHUNK - 1 - i if backward else i), SEGS, stride=pitch)
                carried = [steps[k] * carried[k] for k in range(poles)]
                total_ref[row, :] = add_up([*carried, local_ref[h, row, :]])
            return tuple(
                carried[k]
                + weights[k]
                * chunk_ref[h, pl.ds(pl.multiple_of((m * poles + k) * SEGS, SEGS), SEGS), :]
                for k in range(poles)
            )

        lax.fori_loop(0, chunks, body, carried, unroll=2)

        def gate(q, _):
            whole = total_ref[pl.ds(pl.multiple_of(q * pitch, 8), seg_len), :]
            rows = pl.ds(pl.multiple_of(q * seg_len, STEP), seg_len)
            for gate_ref, target in zip(gates, targets):
                target[rows, lanes] = (gate_ref[rows, lanes].astype(F32) * whole).astype(BF16)
            return _

        for part in range(PIECES):
            first, last = part * SEGS // PIECES, (part + 1) * SEGS // PIECES
            lax.fori_loop(first, last, gate, 0, unroll=4)
            send(h, part, pl.ds(first * seg_len, (last - first) * seg_len), lanes)


def finish_kernel(
    seg_len,
    blocks,
    settled,
    outer_ref,
    inner_ref,
    values_ref,
    cotangent_ref,
    ahead_ref,
    back_ref,
    gain_ref,
    loss_ref,
    ends_ref,
    starts_ref,
    table_ref,
    entry_ref,
    *rest,
):
    if settled:
        out_a, out_b, state_ref, total_ref = rest
    else:
        shift_ref, other_ref, done_a, done_b, *outs, out_a, out_b, state_ref, total_ref, done_sems, out_sems = rest
    later = lax.axis_index("ctx") >= blocks // 2

    def run(backward):
        copies = []
        if not settled:
            here = (2, 3) if backward else (0, 1)
            there = (0, 1) if backward else (2, 3)
            for j, ready in enumerate((done_a, done_b)):
                copy = pltpu.make_async_copy(ready, outs[there[j]], done_sems.at[j])
                copy.start()
                copies.append(copy)

        def send(h, part, rows, lanes):
            if settled:
                return
            for j, ready in enumerate((out_a, out_b)):
                copy = pltpu.make_async_copy(
                    ready.at[rows, lanes], outs[here[j]].at[rows, lanes], out_sems.at[h, part, j]
                )
                copy.start()
                copies.append(copy)

        def entry(lanes):
            if settled:
                return entry_ref[:, lanes]
            return entry_ref[:, lanes] + shift_ref[:, lanes] * other_ref[:, lanes]

        if backward:
            gates = (values_ref, inner_ref)
            parts = (back_ref, loss_ref, starts_ref)
        else:
            gates = (outer_ref, cotangent_ref)
            parts = (ahead_ref, gain_ref, ends_ref)
        finish_way(
            seg_len,
            backward,
            gates,
            *parts,
            table_ref,
            entry,
            (out_a, out_b),
            state_ref,
            total_ref,
            send,
        )
        for copy in copies:
            copy.wait()

    pl.when(later)(functools.partial(run, settled))
    pl.when(jnp.logical_not(later))(functools.partial(run, not settled))


def shards(outer_gate, inner_gate, values, cotangent, residue, decay_rate, skip_gain):
    rows, channels = values.shape
    poles = residue.shape[1]
    seg_len = rows // SEGS
    padded = SEGS * (seg_len + PAD)
    count = channels // LANES
    blocks = lax.axis_size("ctx")
    levels = blocks.bit_length() - 1
    gate = jax.ShapeDtypeStruct((rows, channels), BF16)
    limit = pltpu.CompilerParams(vmem_limit_bytes=4 << 20)
    work = rows * channels * poles
    dma = pltpu.SemaphoreType.DMA

    def in_hbm(x):
        return pltpu.with_memory_space_constraint(x, pltpu.HBM)

    arrays = [in_hbm(x) for x in (outer_gate, inner_gate, values, cotangent)]
    mixed, grad, gain, loss, ends, starts, own, table, factors, *gates = pl.pallas_call(
        functools.partial(state_kernel, seg_len, blocks),
        out_shape=[jax.ShapeDtypeStruct((count, padded, LANES), F32)] * 2
        + [jax.ShapeDtypeStruct((count, rows // CHUNK * poles, LANES), F32)] * 2
        + [jax.ShapeDtypeStruct((count, SEGS * poles, LANES), F32)] * 2
        + [jax.ShapeDtypeStruct((2 * poles, channels), F32)] * 2
        + [jax.ShapeDtypeStruct((6 * poles, channels), F32)]
        + [gate] * 4,
        in_specs=[HBM] * 6,
        out_specs=[VMEM] * 13,
        scratch_shapes=[dma((count, 4)), dma((2,))],
        compiler_params=limit,
        name="states",
    )(*arrays, in_hbm(decay_rate.T), in_hbm(residue.T))
    skip = skip_gain[None, :]

    def local(signal, backward, held):
        signal, _ = lax.optimization_barrier((signal, held))
        shapes = [jax.ShapeDtypeStruct(signal.shape, F32)]
        if not backward:
            shapes.append(jax.ShapeDtypeStruct((6 * (levels - 2) * poles + 2 * poles, channels), F32))
        return pl.pallas_call(
            functools.partial(local_kernel, seg_len, blocks, backward),
            out_shape=shapes,
            in_specs=[VMEM] * 3,
            out_specs=[VMEM] * len(shapes),
            input_output_aliases={0: 0},
            compiler_params=limit,
            cost_estimate=pl.CostEstimate(
                flops=rows * channels * 17, bytes_accessed=signal.size * 8, transcendentals=0
            ),
            name="local",
        )(signal, table, skip)

    def partners(bit):
        return [(i, i ^ (1 << bit) ^ (1 if bit else 0)) for i in range(blocks)]

    jobs = [(mixed, False), (grad, True)]
    found = []
    entry = jnp.zeros_like(own)
    for bit in range(levels - 1):
        other = lax.ppermute(own, "ctx", partners(bit))
        pieces = []
        if bit and jobs:
            piece, *more = local(*jobs.pop(0), own)
            pieces = [piece]
            factors = more[0] if more else factors
        base = 6 * max(bit - 1, 0) * poles
        keep, take, join = factors[base : base + 6 * poles].reshape(3, 2 * poles, channels)
        entry = entry + join * other
        own = keep * own + take * other
        own, entry, pieces = lax.optimization_barrier((own, entry, pieces))
        found += pieces
    for job in jobs:
        piece, *more = local(*job, own)
        found.append(piece)
        factors = more[0] if more else factors
    shift, late = factors[-2 * poles :].reshape(2, poles, channels)

    def choose(when_later, otherwise):
        return late * when_later + (1.0 - late) * otherwise

    ahead, back = own[:poles], own[poles:]
    ahead_entry, back_entry = entry[:poles], entry[poles:]
    sent, shift, settled_entry, open_entry = lax.optimization_barrier(
        (
            choose(back, ahead),
            shift,
            choose(back_entry, ahead_entry),
            choose(ahead_entry, back_entry),
        )
    )
    other = lax.ppermute(sent, "ctx", partners(levels - 1))

    def finish(settled, entry, before):
        work_space = [pltpu.VMEM((SEGS * poles, LANES), F32), pltpu.VMEM((padded, LANES), F32)]
        if not settled:
            work_space = [pltpu.VMEM((rows, channels), BF16)] * 2 + work_space
            work_space += [dma((2,)), dma((count, PIECES, 2))]
        return pl.pallas_call(
            functools.partial(finish_kernel, seg_len, blocks, settled),
            out_shape=[gate] * (2 if settled else 4),
            in_specs=[VMEM] * (12 + len(before)),
            out_specs=[VMEM] * 2 if settled else [HBM] * 4,
            scratch_shapes=work_space,
            compiler_params=limit,
            cost_estimate=pl.CostEstimate(
                flops=work * 2, bytes_accessed=rows * channels * 12, transcendentals=0
            ),
            name="settled" if settled else "last",
        )(*gates, *found, gain, loss, ends, starts, table, entry, *before)

    ready = finish(True, settled_entry, ())
    other, ready = lax.optimization_barrier((other, ready))
    return finish(False, open_entry, (shift, other, *ready))


def solution(mesh):
    spread = P(("groups", "ctx"), None)
    return jax.shard_map(
        shards,
        mesh=mesh,
        in_specs=(spread,) * 4 + (P(),) * 3,
        out_specs=(spread,) * 4,
        check_vma=False,
    )
```

```python
import functools
import jax
import jax.numpy as jnp
from jax import lax
from jax.experimental import pallas as pl
from jax.experimental.pallas import tpu as pltpu
from jax.sharding import PartitionSpec as P

SEGS = 8
LANES = 128
PAD = 8
STEP = 16
CHUNK = 16
PIECES = 2
F32 = jnp.float32
BF16 = jnp.bfloat16
VMEM = pl.BlockSpec(memory_space=pltpu.VMEM)
HBM = pl.BlockSpec(memory_space=pltpu.HBM)


def lane_slice(half):
    return slice(half * LANES, (half + 1) * LANES)


def add_up(terms):
    while len(terms) > 1:
        odd = [terms[-1]] if len(terms) % 2 else []
        terms = [a + b for a, b in zip(terms[::2], terms[1::2])] + odd
    return terms[0]


def spread_rows(table, lanes, count):
    return [jnp.broadcast_to(table[k : k + 1, lanes], (8, LANES)) for k in range(count)]


def factor_tables(rates, rows, blocks, bits, factor_ref):
    poles, channels = rates.shape
    me = lax.axis_index("ctx")
    one = jnp.ones((poles, channels), F32)
    zero = jnp.zeros((poles, channels), F32)
    base = 0
    for bit in bits:
        reach = 1 << bit
        later = jnp.bitwise_and(jnp.right_shift(me, bit), 1) == 1
        place = jnp.bitwise_and(me, reach - 1)
        gap = jnp.where(later, place, reach - 1 - place).astype(F32)
        shift = jnp.exp(-rates * (float(rows) * gap))
        if 2 * reach < blocks:
            span = jnp.exp(-float(rows * reach) * rates)
            first, second = jnp.where(later, one, span), jnp.where(later, span, one)
            parts = (first, second, second, first)
            parts += (jnp.where(later, shift, zero), jnp.where(later, zero, shift))
        else:
            parts = (shift, jnp.where(later, one, zero))
        for part in parts:
            factor_ref[base : base + poles, :] = part
            base += poles


def state_kernel(
    seg_len,
    blocks,
    outer_hbm,
    inner_hbm,
    values_hbm,
    cotangent_hbm,
    rate_hbm,
    residue_hbm,
    mixed_ref,
    grad_ref,
    gain_ref,
    loss_ref,
    ends_ref,
    starts_ref,
    own_ref,
    table_ref,
    factor_ref,
    outer_ref,
    inner_ref,
    values_ref,
    cotangent_ref,
    copy_sems,
    table_sems,
):
    poles = rate_hbm.shape[0]
    pitch = seg_len + PAD
    count = mixed_ref.shape[0]
    chunks = seg_len // CHUNK
    pairs = (
        (inner_hbm, inner_ref),
        (values_hbm, values_ref),
        (outer_hbm, outer_ref),
        (cotangent_hbm, cotangent_ref),
    )
    copies = [
        [
            pltpu.make_async_copy(
                source.at[:, lane_slice(h)], target.at[:, lane_slice(h)], copy_sems.at[h, j]
            )
            for j, (source, target) in enumerate(pairs)
        ]
        for h in range(count)
    ]
    tables = [
        pltpu.make_async_copy(
            source, table_ref.at[pl.ds(j * poles, poles), :], table_sems.at[j]
        )
        for j, source in enumerate((rate_hbm, residue_hbm))
    ]
    first = copies[0][:2]
    for copy in first + tables + copies[0][2:]:
        copy.start()
    for h in range(count):
        lanes = lane_slice(h)

        def convert(first_ref, second_ref, target_ref, rounded):
            def segment(q, _):
                source = pl.ds(pl.multiple_of(q * seg_len, STEP), seg_len)
                target = pl.ds(pl.multiple_of(q * pitch, 8), seg_len)
                first, second = first_ref[source, lanes], second_ref[source, lanes]
                if rounded:
                    product = (first * second).astype(F32)
                else:
                    product = first.astype(F32) * second.astype(F32)
                target_ref[h, target, :] = product
                return _

            lax.fori_loop(0, SEGS, segment, 0, unroll=8)

        def sums(signal_ref, chunk_ref, backward):
            steps = spread_rows(decay, lanes, poles)

            def chunk(m, _):
                for j in range(CHUNK):
                    row = m * CHUNK + (CHUNK - 1 - j if backward else j)
                    x = signal_ref[h, pl.ds(row, SEGS, stride=pitch), :]
                    state = [steps[k] * state[k] + x for k in range(poles)] if j else [x] * poles
                for k in range(poles):
                    rows = pl.ds(pl.multiple_of((m * poles + k) * SEGS, SEGS), SEGS)
                    chunk_ref[h, rows, :] = state[k]
                return _

            lax.fori_loop(0, chunks, chunk, 0, unroll=8)

        for copy in copies[h][:2]:
            copy.wait()
        if h == 0:
            for line in copies[1:]:
                for copy in line:
                    copy.start()
        convert(inner_ref, values_ref, mixed_ref, True)
        if h == 0:
            for copy in tables:
                copy.wait()
            rate_table = table_ref[0:poles, :]
            decay = jnp.exp(-rate_table)
            chunk_decay = jnp.exp(-float(CHUNK) * rate_table)
            seg_decay = jnp.exp(-float(seg_len) * rate_table)
            factor_tables(rate_table, seg_len * SEGS, blocks, range(1), factor_ref)
        sums(mixed_ref, gain_ref, False)
        for copy in copies[h][2:]:
            copy.wait()
        convert(outer_ref, cotangent_ref, grad_ref, False)
        sums(grad_ref, loss_ref, True)
        longer = spread_rows(chunk_decay, lanes, poles)
        for k in range(poles):
            ahead = gain_ref[h, SEGS * k : SEGS * (k + 1), :]
            last = ((chunks - 1) * poles + k) * SEGS
            back = loss_ref[h, last : last + SEGS, :]
            for m in range(1, chunks):
                row = (m * poles + k) * SEGS
                ahead = longer[k] * ahead + gain_ref[h, row : row + SEGS, :]
                row = ((chunks - 1 - m) * poles + k) * SEGS
                back = longer[k] * back + loss_ref[h, row : row + SEGS, :]
            ends_ref[h, SEGS * k : SEGS * (k + 1), :] = ahead
            starts_ref[h, SEGS * k : SEGS * (k + 1), :] = back
        ahead = jnp.zeros((poles, LANES), F32)
        back = jnp.zeros((poles, LANES), F32)
        for q in range(SEGS):
            ahead = seg_decay[:, lanes] * ahead + ends_ref[h, pl.ds(q, poles, stride=SEGS), :]
            back = seg_decay[:, lanes] * back + starts_ref[
                h, pl.ds(SEGS - 1 - q, poles, stride=SEGS), :
            ]
        own_ref[0:poles, lanes] = ahead
        own_ref[poles : 2 * poles, lanes] = back


def local_kernel(seg_len, blocks, backward, signal_ref, table_ref, skip_ref, out_ref, *factor_refs):
    poles = table_ref.shape[0] // 2
    pitch = seg_len + PAD
    chunks = seg_len // CHUNK
    for factor_ref in factor_refs:
        bits = range(1, blocks.bit_length() - 1)
        factor_tables(table_ref[0:poles, :], seg_len * SEGS, blocks, bits, factor_ref)
    weight = table_ref[poles : 2 * poles, :]
    decay = jnp.exp(-table_ref[0:poles, :])
    rows = []
    for lag in range(CHUNK):
        rows.append(jnp.sum(weight, axis=0, keepdims=True))
        weight = weight * decay
    rows[0] = rows[0] + skip_ref[...]
    for h in range(signal_ref.shape[0]):
        lanes = lane_slice(h)
        taps = [jnp.broadcast_to(row[:, lanes], (SEGS, LANES)) for row in rows]

        def fetch(m):
            return tuple(
                signal_ref[h, pl.ds(m * CHUNK + j, SEGS, stride=pitch), :] for j in range(CHUNK)
            )

        def body(m, held):
            following = fetch(jnp.minimum(m + 1, chunks - 1))
            for j in range(CHUNK):
                lags = range(CHUNK - j) if backward else range(j + 1)
                terms = [taps[lag] * held[j + lag if backward else j - lag] for lag in lags]
                out_ref[h, pl.ds(m * CHUNK + j, SEGS, stride=pitch), :] = add_up(terms)
            return following

        lax.fori_loop(0, chunks, body, fetch(0), unroll=2)


def finish_way(
    seg_len,
    backward,
    gates,
    local_ref,
    chunk_ref,
    edge_ref,
    table_ref,
    entry,
    targets,
    state_ref,
    total_ref,
    send,
):
    poles = table_ref.shape[0] // 2
    pitch = seg_len + PAD
    chunks = seg_len // CHUNK
    rates = table_ref[0:poles, :]
    decay = jnp.exp(-rates)
    seg_decay = jnp.exp(-float(seg_len) * rates)
    for h in range(local_ref.shape[0]):
        lanes = lane_slice(h)
        state = entry(lanes)
        for n in range(SEGS):
            q = SEGS - 1 - n if backward else n
            state_ref[pl.ds(q, poles, stride=SEGS), :] = state
            if n < SEGS - 1:
                edge = edge_ref[h, pl.ds(q, poles, stride=SEGS), :]
                state = seg_decay[:, lanes] * state + edge
        steps = spread_rows(decay, lanes, poles)
        weights = spread_rows(table_ref[poles : 2 * poles, :], lanes, poles)
        carried = tuple(
            weights[k] * state_ref[SEGS * k : SEGS * (k + 1), :] for k in range(poles)
        )

        def body(n, carried):
            m = chunks - 1 - n if backward else n
            for i in range(CHUNK):
                row = pl.ds(m * CHUNK + (CHUNK - 1 - i if backward else i), SEGS, stride=pitch)
                carried = [steps[k] * carried[k] for k in range(poles)]
                total_ref[row, :] = add_up([*carried, local_ref[h, row, :]])
            return tuple(
                carried[k]
                + weights[k]
                * chunk_ref[h, pl.ds(pl.multiple_of((m * poles + k) * SEGS, SEGS), SEGS), :]
                for k in range(poles)
            )

        lax.fori_loop(0, chunks, body, carried, unroll=2)

        def gate(q, _):
            whole = total_ref[pl.ds(pl.multiple_of(q * pitch, 8), seg_len), :]
            rows = pl.ds(pl.multiple_of(q * seg_len, STEP), seg_len)
            for gate_ref, target in zip(gates, targets):
                target[rows, lanes] = (gate_ref[rows, lanes].astype(F32) * whole).astype(BF16)
            return _

        for part in range(PIECES):
            first, last = part * SEGS // PIECES, (part + 1) * SEGS // PIECES
            lax.fori_loop(first, last, gate, 0, unroll=4)
            send(h, part, pl.ds(first * seg_len, (last - first) * seg_len), lanes)


def finish_kernel(
    seg_len,
    blocks,
    settled,
    outer_ref,
    inner_ref,
    values_ref,
    cotangent_ref,
    ahead_ref,
    back_ref,
    gain_ref,
    loss_ref,
    ends_ref,
    starts_ref,
    table_ref,
    entry_ref,
    *rest,
):
    if settled:
        out_a, out_b, state_ref, total_ref = rest
    else:
        shift_ref, other_ref, done_a, done_b, *outs, out_a, out_b, state_ref, total_ref, done_sems, out_sems = rest
    later = lax.axis_index("ctx") >= blocks // 2

    def run(backward):
        copies = []
        if not settled:
            here = (2, 3) if backward else (0, 1)
            there = (0, 1) if backward else (2, 3)
            for j, ready in enumerate((done_a, done_b)):
                copy = pltpu.make_async_copy(ready, outs[there[j]], done_sems.at[j])
                copy.start()
                copies.append(copy)

        def send(h, part, rows, lanes):
            if settled:
                return
            for j, ready in enumerate((out_a, out_b)):
                copy = pltpu.make_async_copy(
                    ready.at[rows, lanes], outs[here[j]].at[rows, lanes], out_sems.at[h, part, j]
                )
                copy.start()
                copies.append(copy)

        def entry(lanes):
            if settled:
                return entry_ref[:, lanes]
            return entry_ref[:, lanes] + shift_ref[:, lanes] * other_ref[:, lanes]

        if backward:
            gates = (values_ref, inner_ref)
            parts = (back_ref, loss_ref, starts_ref)
        else:
            gates = (outer_ref, cotangent_ref)
            parts = (ahead_ref, gain_ref, ends_ref)
        finish_way(
            seg_len,
            backward,
            gates,
            *parts,
            table_ref,
            entry,
            (out_a, out_b),
            state_ref,
            total_ref,
            send,
        )
        for copy in copies:
            copy.wait()

    pl.when(later)(functools.partial(run, settled))
    pl.when(jnp.logical_not(later))(functools.partial(run, not settled))


def shards(outer_gate, inner_gate, values, cotangent, residue, decay_rate, skip_gain):
    rows, channels = values.shape
    poles = residue.shape[1]
    seg_len = rows // SEGS
    padded = SEGS * (seg_len + PAD)
    count = channels // LANES
    blocks = lax.axis_size("ctx")
    levels = blocks.bit_length() - 1
    gate = jax.ShapeDtypeStruct((rows, channels), BF16)
    limit = pltpu.CompilerParams(vmem_limit_bytes=4 << 20)
    work = rows * channels * poles
    dma = pltpu.SemaphoreType.DMA

    def in_hbm(x):
        return pltpu.with_memory_space_constraint(x, pltpu.HBM)

    arrays = [in_hbm(x) for x in (outer_gate, inner_gate, values, cotangent)]
    mixed, grad, gain, loss, ends, starts, own, table, factors, *gates = pl.pallas_call(
        functools.partial(state_kernel, seg_len, blocks),
        out_shape=[jax.ShapeDtypeStruct((count, padded, LANES), F32)] * 2
        + [jax.ShapeDtypeStruct((count, rows // CHUNK * poles, LANES), F32)] * 2
        + [jax.ShapeDtypeStruct((count, SEGS * poles, LANES), F32)] * 2
        + [jax.ShapeDtypeStruct((2 * poles, channels), F32)] * 2
        + [jax.ShapeDtypeStruct((6 * poles, channels), F32)]
        + [gate] * 4,
        in_specs=[HBM] * 6,
        out_specs=[VMEM] * 13,
        scratch_shapes=[dma((count, 4)), dma((2,))],
        compiler_params=limit,
        name="states",
    )(*arrays, in_hbm(decay_rate.T), in_hbm(residue.T))
    skip = skip_gain[None, :]

    def local(signal, backward, held):
        signal, _ = lax.optimization_barrier((signal, held))
        shapes = [jax.ShapeDtypeStruct(signal.shape, F32)]
        if not backward:
            shapes.append(jax.ShapeDtypeStruct((6 * (levels - 2) * poles + 2 * poles, channels), F32))
        return pl.pallas_call(
            functools.partial(local_kernel, seg_len, blocks, backward),
            out_shape=shapes,
            in_specs=[VMEM] * 3,
            out_specs=[VMEM] * len(shapes),
            input_output_aliases={0: 0},
            compiler_params=limit,
            cost_estimate=pl.CostEstimate(
                flops=rows * channels * 17, bytes_accessed=signal.size * 8, transcendentals=0
            ),
            name="local",
        )(signal, table, skip)

    def partners(bit):
        return [(i, i ^ (1 << bit) ^ (1 if bit else 0)) for i in range(blocks)]

    jobs = [(mixed, False), (grad, True)]
    found = []
    entry = jnp.zeros_like(own)
    for bit in range(levels - 1):
        other = lax.ppermute(own, "ctx", partners(bit))
        pieces = []
        if bit and jobs:
            piece, *more = local(*jobs.pop(0), own)
            pieces = [piece]
            factors = more[0] if more else factors
        base = 6 * max(bit - 1, 0) * poles
        keep, take, join = factors[base : base + 6 * poles].reshape(3, 2 * poles, channels)
        entry = entry + join * other
        own = keep * own + take * other
        own, entry, pieces = lax.optimization_barrier((own, entry, pieces))
        found += pieces
    for job in jobs:
        piece, *more = local(*job, own)
        found.append(piece)
        factors = more[0] if more else factors
    shift, late = factors[-2 * poles :].reshape(2, poles, channels)

    def choose(when_later, otherwise):
        return late * when_later + (1.0 - late) * otherwise

    ahead, back = own[:poles], own[poles:]
    ahead_entry, back_entry = entry[:poles], entry[poles:]
    sent, shift, settled_entry, open_entry = lax.optimization_barrier(
        (
            choose(back, ahead),
            shift,
            choose(back_entry, ahead_entry),
            choose(ahead_entry, back_entry),
        )
    )
    other = lax.ppermute(sent, "ctx", partners(levels - 1))

    def finish(settled, entry, before):
        work_space = [pltpu.VMEM((SEGS * poles, LANES), F32), pltpu.VMEM((padded, LANES), F32)]
        if not settled:
            work_space = [pltpu.VMEM((rows, channels), BF16)] * 2 + work_space
            work_space += [dma((2,)), dma((count, PIECES, 2))]
        return pl.pallas_call(
            functools.partial(finish_kernel, seg_len, blocks, settled),
            out_shape=[gate] * (2 if settled else 4),
            in_specs=[VMEM] * (12 + len(before)),
            out_specs=[VMEM] * 2 if settled else [HBM] * 4,
            scratch_shapes=work_space,
            compiler_params=limit,
            cost_estimate=pl.CostEstimate(
                flops=work * 2, bytes_accessed=rows * channels * 12, transcendentals=0
            ),
            name="settled" if settled else "last",
        )(*gates, *found, gain, loss, ends, starts, table, entry, *before)

    ready = finish(True, settled_entry, ())
    other, ready = lax.optimization_barrier((other, ready))
    return finish(False, open_entry, (shift, other, *ready))


def solution(mesh):
    spread = P(("groups", "ctx"), None)
    return jax.shard_map(
        shards,
        mesh=mesh,
        in_specs=(spread,) * 4 + (P(),) * 3,
        out_specs=(spread,) * 4,
        check_vma=False,
    )
```
